256 devices in a mesh: rows: 64 (over z, y, x_lo), cols: 4 (over x_hi, core).
Axes of the slice: x: 4 (x_hi: 2, x_lo: 2; x = x_hi * 2 + x_lo), y: 4, z: 8, core: 2. Of those that a mesh axis runs over, the one named last changes fastest.
Arguments:
- h_start: float32 [32768, 128], P(('rows', 'cols')), may hold values from -6 to 6
- cotangent: float32 [32768, 128], P(('rows', 'cols')), may hold values from -6 to 6
- node_type: int32 [32768], P(('rows', 'cols')), may hold values from 0 to 7
- teleport: float32 [8], replicated, may hold values from 0.05 to 0.5
- tile_values: bfloat16 [64, 4, 192, 128, 128], P('rows', 'cols'), may hold values from -0.0390625 to 0.0390625
- tile_row: int32 [64, 4, 192], P('rows', 'cols'), may hold values from 0 to 3, as said below
- tile_col: int32 [64, 4, 192], P('rows', 'cols'), may hold values from 0 to 63
- tile_count: int32 [64, 4], P('rows', 'cols'), may hold values from 24 to 192, as said below
Outputs:
- propagated: float32 [32768, 128], P(('rows', 'cols'))
- input_grad: float32 [32768, 128], P(('rows', 'cols'))
The draws below stay inside these ranges and needn't reach their ends.
Inputs may be any that keep to these rules, and one draw needn't show every extreme that they name: Within one row block and column range, the pairs (tile_row, tile_col) of the 192 slots are all different. `tile_count`: slots at or beyond the count are not part of A. In every draw 4 row blocks use all 192 slots in every column range.
All inputs are finite; a program needn't handle non-finite values.
Results may differ from the reference program's by a relative error of at most 0.0029.
Values may be sent and summed in bfloat16 or wider, within the bound.
A program may use at most 64 MiB of HBM per device.

```python
import math
import jax
import jax.numpy as jnp
from jax import lax

F = 128
TB = 128
TYPES = 8
TILES_DEV = 1
ROW_BLOCKS = 64
RANGES = 4
ROW_TILES = 4
COL_TILES = 64
SLOTS = 192
HUBS = 4
NODES = 32768


def pick_order(single):
    return jax.random.permutation(single, ROW_TILES * COL_TILES)


def tile_layout(key):
    layout_key = jax.random.fold_in(key, 101)
    device_keys = jax.random.split(layout_key, ROW_BLOCKS * RANGES)
    slot_order = jax.vmap(pick_order)(device_keys)[:, :SLOTS]
    slot_order = slot_order.reshape(ROW_BLOCKS, RANGES, SLOTS).astype(jnp.int32)
    return (slot_order // COL_TILES, slot_order % COL_TILES)


def draw_tile_row(key, part):
    return tile_layout(key)[0]


def draw_tile_col(key, part):
    return tile_layout(key)[1]


def draw_tile_count(key, part):
    hub_order = jax.random.permutation(jax.random.fold_in(key, 202), ROW_BLOCKS)
    is_hub = jnp.zeros((ROW_BLOCKS,), jnp.int32).at[hub_order[:HUBS]].set(1)
    light_count = jax.random.randint(jax.random.fold_in(key, 303), (ROW_BLOCKS, RANGES), SLOTS // 8, SLOTS // 2 + 1, dtype=jnp.int32)
    return jnp.where(is_hub[:, None] == 1, SLOTS, light_count).astype(jnp.int32)


def place_ends(array, stream_key, least, high):
    index_at = [jax.random.randint(jax.random.fold_in(stream_key, axis), (), 0, length) for axis, length in enumerate(array.shape)]
    widest = array.shape.index(max(array.shape))
    next_to = index_at[:widest] + [(index_at[widest] + 1) % array.shape[widest]] + index_at[widest + 1:]
    return array.at[tuple(index_at)].set(least).at[tuple(next_to)].set(high)


def steps_of(own_key, extent, cuts, least, largest):
    def one(position, parts):
        heights = jax.random.uniform(jax.random.fold_in(jax.random.fold_in(own_key, 6), position), (parts,), jnp.float32, least / len(cuts), largest / len(cuts))
        return jnp.repeat(jnp.exp(heights), extent[position] // parts).reshape((-1,) + (1,) * (len(extent) - position - 1))

    factor_of = one(*cuts[0])
    for cut in cuts[1:]:
        factor_of = factor_of * one(*cut)
    return factor_of


def noise(rng, shape, width, most, cuts=(), held_as=jnp.bfloat16):
    loudness = steps_of(rng, shape, cuts, -0.22, 0.18) if cuts else 1.0
    drawn = jax.random.normal(rng, shape, jnp.float32) * width * loudness
    return jnp.minimum(jnp.maximum(drawn, -most), most).astype(held_as)


def setup_inputs(seed: int = 0) -> dict:
    splits = jax.random.split(jax.random.key(seed), 9)
    h_start = noise(splits[0], (NODES, F), 1.0, 6.0, ((0, 256),), jnp.float32)
    cotangent = noise(splits[1], (NODES, F), 1.0, 6.0, ((0, 256),), jnp.float32)
    node_type = place_ends(jax.random.randint(splits[2], (NODES,), 0, TYPES), jax.random.fold_in(splits[2], 1), 0, TYPES - 1).astype(jnp.int32)
    teleport = jnp.clip(jnp.exp(jax.random.uniform(splits[3], (TYPES,), jnp.float32, math.log(0.05), math.log(0.5))), 0.05, 0.5)
    tile_values = noise(splits[4], (ROW_BLOCKS, RANGES, SLOTS, TB, TB), (SLOTS * TB // TILES_DEV) ** -0.5, 0.0390625, ((0, 64), (1, 4)))
    tile_row = draw_tile_row(jax.random.fold_in(splits[8], 71), 0)
    tile_col = draw_tile_col(jax.random.fold_in(splits[8], 71), 0)
    tile_count = draw_tile_count(jax.random.fold_in(splits[8], 71), 0)
    return {"h_start": h_start, "cotangent": cotangent, "node_type": node_type, "teleport": teleport, "tile_values": tile_values, "tile_row": tile_row, "tile_col": tile_col, "tile_count": tile_count}


def column_tiles(col_index):
    range_ids = jnp.arange(RANGES, dtype=jnp.int32)[:, None]
    return (col_index // TILES_DEV * RANGES + range_ids) * TILES_DEV + col_index % TILES_DEV


def active_slots(tile_count, block_id):
    slot_ids = jnp.arange(SLOTS, dtype=jnp.int32)[None, :]
    return (slot_ids < tile_count[block_id][:, None]).astype(jnp.float32)


def forward_product(panel, tile_values, tile_row, tile_col, tile_count):
    panel_tiles = panel.reshape(NODES // TB, TB, F)

    def one_block(block_id):
        tile_block = tile_values[block_id].astype(jnp.float32)
        row_index = tile_row[block_id]
        col_index = tile_col[block_id]
        active = active_slots(tile_count, block_id)
        fetched = panel_tiles[column_tiles(col_index)].astype(jnp.float32)
        product = jnp.einsum("csij,csjf->csif", tile_block, fetched)
        row_onehot = (row_index[:, :, None] == jnp.arange(ROW_TILES, dtype=jnp.int32)[None, None, :]).astype(jnp.float32)
        row_onehot = row_onehot * active[:, :, None]
        return jnp.einsum("csq,csif->qif", row_onehot, product)

    result = lax.map(one_block, jnp.arange(ROW_BLOCKS, dtype=jnp.int32))
    return result.reshape(NODES, F)


def adjoint_product(adjoint, tile_values, tile_row, tile_col, tile_count):
    adjoint_tiles = adjoint.reshape(NODES // TB, TB, F)

    def advance(running, block_id):
        tile_block = tile_values[block_id].astype(jnp.float32)
        row_index = tile_row[block_id]
        col_index = tile_col[block_id]
        active = active_slots(tile_count, block_id)
        rows_block = lax.dynamic_slice_in_dim(adjoint_tiles, (block_id * ROW_TILES).astype(jnp.int32), ROW_TILES, 0)
        fetched = rows_block[row_index].astype(jnp.float32)
        product = jnp.einsum("csji,csjf->csif", tile_block, fetched) * active[:, :, None, None]
        targets = column_tiles(col_index).reshape(RANGES * SLOTS)
        running = running.at[targets].add(product.reshape(RANGES * SLOTS, TB, F))
        return running, None

    start = jnp.zeros((NODES // TB, TB, F), jnp.float32)
    running = lax.scan(advance, start, jnp.arange(ROW_BLOCKS, dtype=jnp.int32))[0]
    return running.reshape(NODES, F)


def reference(h_start, cotangent, node_type, teleport, tile_values, tile_row, tile_col, tile_count):
    teleport_rate = teleport[node_type][:, None]
    keep_rate = 1.0 - teleport_rate
    hop_one = keep_rate * forward_product(h_start.astype(jnp.bfloat16), tile_values, tile_row, tile_col, tile_count) + teleport_rate * h_start
    propagated = keep_rate * forward_product(hop_one.astype(jnp.bfloat16), tile_values, tile_row, tile_col, tile_count) + teleport_rate * h_start
    back_one = adjoint_product((keep_rate * cotangent).astype(jnp.bfloat16), tile_values, tile_row, tile_col, tile_count)
    back_two = adjoint_product((keep_rate * back_one).astype(jnp.bfloat16), tile_values, tile_row, tile_col, tile_count)
    input_grad = teleport_rate * cotangent + teleport_rate * back_one + back_two
    return propagated, input_grad
```

```python
import functools

import jax
import jax.numpy as jnp
from jax import lax
from jax.experimental import pallas as pl
from jax.experimental.pallas import tpu as pltpu
from jax.sharding import PartitionSpec as P

MESH = pl.DeviceIdType.MESH
T = 128
NZ, NY = 8, 4
COLS = 4
GROUPS = 16
SLOTS = 192
CODED = True
MSG = jnp.int16 if CODED else jnp.float32
PAD = 16 if CODED else 0


def rem(a, n):
    return lax.rem(a + 2 * n, n)


def message_rows():
    offsets, total = {}, 0
    for name, steps, rows in (("az", NZ // 2, 4 * T), ("by", NY // 2, 8 * T), ("bz", NZ // 2, T), ("ay", NY // 2, T), ("x", 1, T)):
        for step in range(1, steps + 1):
            size = rows // 2 if (step == 1 and steps > 1) else rows
            offsets[name, step] = total
            total += size + PAD
    return offsets, total


OFFSETS, MSG_ROWS = message_rows()


def kernel(
    inv, tiles, h, cot, t_col, t_row, prop, grad,
    tv, ad, panel, part, qcat, acc, fsend1, frecv1, fsend2, frecv2, sbuf, rbuf, d_one,
    load_sem, ssem, rsem,
):
    r = lax.axis_index("rows")
    c = lax.axis_index("cols")
    z, y, x = r // 8, lax.rem(r // 2, 4), lax.rem(r, 2)
    xh, core = c // 2, lax.rem(c, 2)

    def at(zz, yy, xx):
        return {"rows": zz * 8 + yy * 2 + xx, "cols": c}

    zp, zm = at(rem(z + 1, NZ), y, x), at(rem(z - 1, NZ), y, x)
    yp, ym = at(z, rem(y + 1, NY), x), at(z, rem(y - 1, NY), x)
    xo = at(z, y, 1 - x)
    c_core = {"rows": r, "cols": xh * 2 + 1 - core}
    c_xh = {"rows": r, "cols": (1 - xh) * 2 + core}
    c_far = {"rows": r, "cols": (1 - xh) * 2 + 1 - core}

    load = pltpu.make_async_copy(tiles, tv.at[pl.ds(0, SLOTS)], load_sem)
    load.start()

    barrier = pltpu.get_barrier_semaphore()
    for peer in (zp, zm, yp, ym, xo, c_core, c_xh, c_far):
        pl.semaphore_signal(barrier, inc=1, device_id=peer, device_id_type=MESH)
    pl.semaphore_wait(barrier, 8)

    counter = [0]
    sent = []

    def remote(src, dst, peer):
        k = counter[0]
        counter[0] += 1
        copy = pltpu.make_async_remote_copy(
            src_ref=src, dst_ref=dst, send_sem=ssem.at[k], recv_sem=rsem.at[k],
            device_id=peer, device_id_type=MESH,
        )
        sent.append(copy)
        return copy

    own = jnp.where(x == 0, z * 4 + y, 32 + y * 8 + z)
    other = jnp.where(x == 0, 32 + y * 8 + z, z * 4 + y)

    def rows_of(start, size):
        return pl.ds(pl.multiple_of(start, 64), size)

    class Gather:
        def __init__(self, buf, n, pos, base, rows, plus, minus):
            self.buf, self.n, self.pos, self.base, self.rows = buf, n, pos, base, rows
            self.plus, self.minus, self.steps, self.waits = plus, minus, n // 2, {}

        def span(self, block, half):
            start = self.base + rem(block, self.n) * self.rows
            if half is None:
                return self.buf.at[rows_of(start, self.rows)]
            size = self.rows // 2
            return self.buf.at[rows_of(start + half * size, size)]

        def start(self, s):
            last = s == self.steps
            up = self.span(self.pos - (s - 1), 0 if last else None)
            down = self.span(self.pos + (s - 1), 1 if last else None)
            a, b = remote(up, up, self.plus), remote(down, down, self.minus)
            a.start()
            b.start()
            self.waits[s] = (a, b)

        def wait(self, s):
            for copy in self.waits[s]:
                copy.wait_recv()

    class Reduce:
        def __init__(self, hop, name, n, pos, base, rows, plus, minus):
            self.hop, self.name, self.n, self.pos, self.base, self.rows = hop, name, n, pos, base, rows
            self.plus, self.minus, self.steps, self.waits = plus, minus, n // 2, {}

        def start_row(self, block, half):
            return self.base + rem(block, self.n) * self.rows + (0 if half is None else half * (self.rows // 2))

        def send(self, s):
            s_rows = self.rows // 2 if s == 1 else self.rows
            off = OFFSETS[self.name, s]
            copies = []
            if s > 1:
                for copy in self.waits[s - 1]:
                    copy.wait_recv()
            for way, peer in ((0, self.minus), (1, self.plus)):
                block = self.pos - (self.steps + 1 - s) if way == 0 else self.pos + (self.steps + 1 - s)
                row = self.start_row(block, way if s == 1 else None)
                if s > 1:
                    p_rows = self.rows // 2 if s == 2 else self.rows
                    p_row = self.start_row(block, way if s == 2 else None)
                    add_message(self.hop, way, OFFSETS[self.name, s - 1], p_row, p_rows)
                pack_message(self.hop, way, off, row, s_rows)
                size = s_rows + PAD
                copy = remote(sbuf.at[self.hop, way, pl.ds(off, size)], rbuf.at[self.hop, way, pl.ds(off, size)], peer)
                copy.start()
                copies.append(copy)
            self.waits[s] = copies

        def finish(self):
            for way, copy in enumerate(self.waits[self.steps]):
                copy.wait_recv()
                add_message(self.hop, way, OFFSETS[self.name, self.steps], self.start_row(self.pos, None), self.rows)

    def add_message(hop, way, off, row, rows):
        step = min(rows, T)
        if CODED:
            e = rbuf[hop, way, pl.ds(off + rows, 16), :].astype(jnp.int32).astype(jnp.float32)
            scale = jnp.exp2(e - 14.0)[None, 0:8, :]

        def one(i, carry):
            src = rbuf[hop, way, pl.ds(pl.multiple_of(off + i * step, 16), step), :]
            if CODED:
                val = src.astype(jnp.int32).astype(jnp.float32).reshape(step // 8, 8, T) * scale
                val = val.reshape(step, T)
            else:
                val = src
            where = rows_of(row + i * step, step)
            part[where, :] = part[where, :] + val
            return carry

        lax.fori_loop(0, rows // step, one, 0)

    def pack_message(hop, way, off, row, rows):
        step = min(rows, T)
        if CODED:
            def largest(i, m):
                a = jnp.abs(part[rows_of(row + i * step, step), :]).reshape(step // 8, 8, T)
                return jnp.maximum(m, jnp.max(a, axis=0))

            m = lax.fori_loop(0, rows // step, largest, jnp.full((8, T), 1e-30, jnp.float32))
            m = jnp.max(m, axis=0, keepdims=True)
            e = jnp.ceil(jnp.log2(m))
            scale = jnp.broadcast_to(jnp.exp2(14.0 - e), (8, T))[None]
            sbuf[hop, way, pl.ds(off + rows, 16), :] = jnp.broadcast_to(e, (16, T)).astype(jnp.int32).astype(jnp.int16)

        def one(i, carry):
            a = part[rows_of(row + i * step, step), :]
            if CODED:
                a = jnp.round(a.reshape(step // 8, 8, T) * scale).reshape(step, T)
                a = a.astype(jnp.int32).astype(jnp.int16)
            sbuf[hop, way, pl.ds(pl.multiple_of(off + i * step, 16), step), :] = a
            return carry

        lax.fori_loop(0, rows // step, one, 0)

    def product_adjoint(hop, group):
        res = jnp.dot(qcat[hop], ad[group], preferred_element_type=jnp.float32)
        for i in range(4):
            part[rows_of(group * 512 + i * T, T), :] = res[:, i * T:(i + 1) * T]

    def product_forward(hop, group):
        acc[...] += jnp.dot(
            ad[group], panel[hop, rows_of(group * 512, 512), :], preferred_element_type=jnp.float32
        )

    def each(fn, hop, groups):
        def one(i, carry):
            g = groups[-1]
            for k in range(len(groups) - 1):
                g = jnp.where(i == k, groups[k], g)
            fn(hop, g)
            return carry

        lax.fori_loop(0, len(groups), one, 0)

    def az_groups(s):
        return [rem(z - s, NZ), rem(z + s, NZ)] if 0 < s < NZ // 2 else [rem(z + s, NZ)]

    def by_groups(s):
        blocks = [rem(y - s, NY), rem(y + s, NY)] if 0 < s < NY // 2 else [rem(y + s, NY)]
        return [8 + 2 * b + i for b in blocks for i in range(2)]

    cot_t = jnp.transpose(cot[...])
    keep_col = 1.0 - t_col[...]
    keep_row = 1.0 - t_row[...]
    lane = pl.ds(pl.multiple_of(c * T, T), T)
    tile_rows = rows_of(own * T, T)
    panel[0, tile_rows, :] = h[...].astype(jnp.bfloat16)
    qcat[0, :, lane] = (keep_row * cot_t).astype(jnp.bfloat16)

    def start_gather(hop):
        buf = panel.at[hop]
        first = remote(buf.at[tile_rows], buf.at[tile_rows], xo)
        first.start()
        return (
            first,
            Gather(buf, NY, y, z * 4 * T, T, yp, ym),
            Gather(buf, NZ, z, (32 + y * 8) * T, T, zp, zm),
            Gather(buf, NZ, z, 0, 4 * T, zp, zm),
            Gather(buf, NY, y, 32 * T, 8 * T, yp, ym),
        )

    def start_cols(hop):
        copies = []
        for peer in (c_core, c_xh, c_far):
            copy = remote(qcat.at[hop, :, lane], qcat.at[hop, :, lane], peer)
            copy.start()
            copies.append(copy)
        return copies

    for hop in range(2):
        first, g_ay, g_bz, g_az, g_by = start_gather(hop)
        q_copies = start_cols(hop)
        az = Reduce(hop, "az", NZ, z, 0, 4 * T, zp, zm)
        by = Reduce(hop, "by", NY, y, 32 * T, 8 * T, yp, ym)
        bz = Reduce(hop, "bz", NZ, z, (32 + y * 8) * T, T, zp, zm)
        ay = Reduce(hop, "ay", NY, y, z * 4 * T, T, yp, ym)

        if hop == 0:
            load.wait()
            tv[SLOTS] = jnp.zeros((T, T), jnp.bfloat16)

            def fill(g, carry):
                for q in range(COLS):
                    for i in range(4):
                        ad[g, q * T:(q + 1) * T, i * T:(i + 1) * T] = tv[inv[q * 64 + g * 4 + i]]
                return carry

            lax.fori_loop(0, GROUPS, fill, 0)
        acc[...] = jnp.zeros_like(acc)

        first.wait_recv()
        g_ay.start(1)
        g_bz.start(1)
        for copy in q_copies:
            copy.wait_recv()
        each(product_adjoint, hop, az_groups(4) + by_groups(2))
        az.send(1)
        by.send(1)
        g_ay.wait(1)
        g_ay.start(2)
        g_bz.wait(1)
        g_bz.start(2)
        each(product_adjoint, hop, az_groups(3) + by_groups(1))
        az.send(2)
        by.send(2)
        g_ay.wait(2)
        g_az.start(1)
        g_bz.wait(2)
        g_bz.start(3)
        each(product_adjoint, hop, az_groups(2) + by_groups(0))
        az.send(3)
        by.finish()
        bz.send(1)
        g_az.wait(1)
        g_az.start(2)
        g_bz.wait(3)
        g_bz.start(4)
        each(product_adjoint, hop, az_groups(1) + az_groups(0))
        az.send(4)
        bz.send(2)
        g_bz.wait(4)
        g_by.start(1)
        each(product_forward, hop, az_groups(0) + az_groups(1))
        g_az.wait(2)
        g_az.start(3)
        az.finish()
        ay.send(1)
        bz.send(3)
        each(product_forward, hop, az_groups(2) + by_groups(0))
        g_by.wait(1)
        g_by.start(2)
        g_az.wait(3)
        g_az.start(4)
        ay.send(2)
        bz.send(4)
        each(product_forward, hop, az_groups(3) + by_groups(1))
        ay.finish()
        bz.finish()
        off = OFFSETS["x", 1]
        pack_message(hop, 0, off, other * T, T)
        x_copy = remote(
            sbuf.at[hop, 0, pl.ds(off, T + PAD)], rbuf.at[hop, 0, pl.ds(off, T + PAD)], xo
        )
        x_copy.start()
        g_az.wait(4)
        g_by.wait(2)
        each(product_forward, hop, az_groups(4) + by_groups(2))

        for i in range(2):
            fsend1[hop, i] = acc[rows_of((2 * i + 1 - core) * T, T), :]
        f_core = remote(fsend1.at[hop], frecv1.at[hop], c_core)
        f_core.start()
        x_copy.wait_recv()
        add_message(hop, 0, off, own * T, T)
        d = part[tile_rows, :]
        if hop == 0:
            d_one[...] = d
            qcat[1, :, lane] = (keep_row * d).astype(jnp.bfloat16)
        else:
            grad[...] = jnp.transpose(t_row[...] * cot_t + t_row[...] * d_one[...] + d)
        f_core.wait_recv()
        fsend2[hop] = acc[rows_of((2 * (1 - xh) + core) * T, T), :] + frecv1[hop, 1 - xh]
        f_xh = remote(fsend2.at[hop], frecv2.at[hop], c_xh)
        f_xh.start()
        mine = acc[rows_of((2 * xh + core) * T, T), :] + frecv1[hop, xh]
        f_xh.wait_recv()
        mine = keep_col * (mine + frecv2[hop]) + t_col[...] * h[...]
        if hop == 0:
            panel[1, tile_rows, :] = mine.astype(jnp.bfloat16)
        else:
            prop[...] = mine

    for copy in sent:
        copy.wait_send()


def shards(h_start, cotangent, node_type, teleport, tile_values, tile_row, tile_col, tile_count):
    type_ids = jnp.arange(teleport.shape[0], dtype=jnp.int32)
    rate = jnp.sum(jnp.where(node_type[:, None] == type_ids[None, :], teleport[None, :], 0.0), axis=1)
    t_col = jnp.broadcast_to(rate[:, None], (T, T))
    t_row = rate[None, :]
    k = tile_col[0, 0]
    kz, ky, kx = k // 8, (k // 2) % 4, k % 2
    place = tile_row[0, 0] * 64 + jnp.where(kx == 0, kz * 4 + ky, 32 + ky * 8 + kz)
    slot = jnp.arange(SLOTS, dtype=jnp.int32)
    place = jnp.where(slot < tile_count[0, 0], place, -1)
    hit = place[None, :] == jnp.arange(COLS * 64, dtype=jnp.int32)[:, None]
    inv = SLOTS + jnp.sum(jnp.where(hit, slot[None, :] - SLOTS, 0), axis=1)

    vmem = pl.BlockSpec(memory_space=pltpu.VMEM)
    tile = jax.ShapeDtypeStruct((T, T), jnp.float32)
    copies = 112
    return pl.pallas_call(
        kernel,
        out_shape=(tile, tile),
        in_specs=[pl.BlockSpec(memory_space=pltpu.SMEM), pl.BlockSpec(memory_space=pl.ANY)] + [vmem] * 4,
        out_specs=(vmem, vmem),
        scratch_shapes=[
            pltpu.VMEM((SLOTS + 1, T, T), jnp.bfloat16),
            pltpu.VMEM((GROUPS, 512, 512), jnp.bfloat16),
            pltpu.VMEM((2, 64 * T, T), jnp.bfloat16),
            pltpu.VMEM((64 * T, T), jnp.float32),
            pltpu.VMEM((2, T, COLS * T), jnp.bfloat16),
            pltpu.VMEM((COLS * T, T), jnp.float32),
            pltpu.VMEM((2, 2, T, T), jnp.float32),
            pltpu.VMEM((2, 2, T, T), jnp.float32),
            pltpu.VMEM((2, T, T), jnp.float32),
            pltpu.VMEM((2, T, T), jnp.float32),
            pltpu.VMEM((2, 2, MSG_ROWS, T), MSG),
            pltpu.VMEM((2, 2, MSG_ROWS, T), MSG),
            pltpu.VMEM((T, T), jnp.float32),
            pltpu.SemaphoreType.DMA,
            pltpu.SemaphoreType.DMA((copies,)),
            pltpu.SemaphoreType.DMA((copies,)),
        ],
        compiler_params=pltpu.CompilerParams(
            collective_id=0, has_side_effects=True, vmem_limit_bytes=56 << 20
        ),
    )(inv, tile_values[0, 0], h_start, cotangent, t_col, t_row)


def solution(mesh):
    placed = (
        P(("rows", "cols"), None),
        P(("rows", "cols"), None),
        P(("rows", "cols")),
        P(),
        P("rows", "cols", None, None, None),
        P("rows", "cols", None),
        P("rows", "cols", None),
        P("rows", "cols"),
    )
    return jax.shard_map(
        shards,
        mesh=mesh,
        in_specs=placed,
        out_specs=(P(("rows", "cols"), None), P(("rows", "cols"), None)),
        check_vma=False,
    )
```

```python
import jax
import jax.numpy as jnp
from jax import lax
from jax.experimental import pallas as pl
from jax.experimental.pallas import tpu as pltpu
from jax.sharding import PartitionSpec as P

MESH = pl.DeviceIdType.MESH
T = 128
NZ, NY, NX = 8, 4, 2
COLS = 4
GROUPS = 16
SLOTS = 192
PAD = 16
PARTS = (2, 1, 3, 0)


def rem(a, n):
    return lax.rem(a + 2 * n, n)


def kernel(
    inv, rates, tiles, h, cot, types, prop, grad,
    tv, ad, panel, part, qcat, acc, fsend1, frecv1, fsend2, frecv2,
    s_one, r_one, s_two, r_two, s_x, r_x, s_own, r_own, d_one,
    load_sem, ssem, rsem, so, ro,
):
    r = lax.axis_index("rows")
    c = lax.axis_index("cols")
    z, y, x = r // 8, lax.rem(r // 2, 4), lax.rem(r, 2)
    xh, core = c // 2, lax.rem(c, 2)
    zpair = z // 2

    def at(zz, yy, xx):
        return {"rows": zz * 8 + yy * 2 + xx, "cols": c}

    zp, zm = at(rem(z + 1, NZ), y, x), at(rem(z - 1, NZ), y, x)
    yp, ym = at(z, rem(y + 1, NY), x), at(z, rem(y - 1, NY), x)
    c_core = {"rows": r, "cols": xh * 2 + 1 - core}
    c_xh = {"rows": r, "cols": (1 - xh) * 2 + core}
    c_far = {"rows": r, "cols": (1 - xh) * 2 + 1 - core}
    y_plane = [(dy, dx) for dy in (2, 1, 3, 0) for dx in (1, 0) if dy or dx]

    def in_y(dy, dx):
        return at(z, rem(y + dy, NY), 1 - x if dx else x)

    load = pltpu.make_async_copy(tiles, tv.at[pl.ds(0, SLOTS)], load_sem)
    load.start()

    barrier = pltpu.get_barrier_semaphore()
    peers = [in_y(*p) for p in y_plane] + [at(rem(z + d, NZ), y, x) for d in range(1, NZ)] + [c_core, c_xh, c_far]
    for peer in peers:
        pl.semaphore_signal(barrier, inc=1, device_id=peer, device_id_type=MESH)

    t_row = jnp.zeros((1, T), jnp.float32)
    for i in range(8):
        t_row = t_row + jnp.where(types[...] == i, rates[i], 0.0)
    keep_row = 1.0 - t_row
    lane = pl.ds(pl.multiple_of(c * T, T), T)
    panel[0, z, x, y] = h[...].astype(jnp.bfloat16)
    qcat[0, :, lane] = (keep_row * jnp.transpose(cot[...])).astype(jnp.bfloat16)

    counter = [0]
    sent = []

    def remote(src, dst, peer):
        k = counter[0]
        counter[0] += 1
        copy = pltpu.make_async_remote_copy(
            src_ref=src, dst_ref=dst, send_sem=ssem.at[k], recv_sem=rsem.at[k],
            device_id=peer, device_id_type=MESH,
        )
        copy.index = k
        sent.append(copy)
        return copy

    def landed(slot, copy):
        pltpu.make_async_remote_copy(
            src_ref=slot, dst_ref=slot, send_sem=ssem.at[copy.index], recv_sem=rsem.at[copy.index],
            device_id=yp, device_id_type=MESH,
        ).wait_recv()

    def rows_of(start, size):
        return pl.ds(pl.multiple_of(start, T), size)

    def each(fn, hop, groups):
        def one(i, carry):
            g = groups[-1]
            for k in range(len(groups) - 1):
                g = jnp.where(i == k, groups[k], g)
            fn(hop, g)
            return carry

        lax.fori_loop(0, len(groups), one, 0)

    def tile_row(dy, zz, xx):
        return (rem(y + dy, NY) * 16 + xx * 8 + zz) * T

    def product_adjoint(hop, g):
        res = jnp.dot(qcat[hop], ad[g], preferred_element_type=jnp.float32)
        for i in range(NY):
            part[rows_of((i * 16 + lax.rem(g, 2) * 8 + g // 2) * T, T), :] = res[:, i * T:(i + 1) * T]

    def product_forward(hop, g):
        tile4 = panel[hop, g // 2, lax.rem(g, 2)].reshape(NY * T, T)
        acc[...] += jnp.dot(ad[g], tile4, preferred_element_type=jnp.float32)

    def decode(msg, row, scale):
        val = msg[rows_of(row, T), :].astype(jnp.int32).astype(jnp.float32)
        return (val.reshape(T // 8, 8, T) * scale).reshape(T, T)

    def scale_of(msg, rows):
        e = msg[pl.ds(rows, PAD), :].astype(jnp.int32).astype(jnp.float32)
        return jnp.exp2(e - 14.0)[None, 0:8, :]

    def place(row, i):
        return rows_of(row + (i // 2) * 8 * T + lax.rem(i, 2) * T, T)

    def add_message(msg, row, tiles_in):
        scale = scale_of(msg, tiles_in * T)

        def one(i, carry):
            where = place(row, i)
            part[where, :] = part[where, :] + decode(msg, i * T, scale)
            return carry

        lax.fori_loop(0, tiles_in, one, 0)

    def pack_message(msg, row, tiles_in):
        def largest(i, m):
            a = jnp.abs(part[place(row, i), :]).reshape(T // 8, 8, T)
            return jnp.maximum(m, jnp.max(a, axis=0))

        m = lax.fori_loop(0, tiles_in, largest, jnp.full((8, T), 1e-30, jnp.float32))
        e = jnp.ceil(jnp.log2(jnp.max(m, axis=0, keepdims=True)))
        scale = jnp.broadcast_to(jnp.exp2(14.0 - e), (8, T))[None]
        msg[pl.ds(tiles_in * T, PAD), :] = jnp.broadcast_to(e, (PAD, T)).astype(jnp.int32).astype(jnp.int16)

        def one(i, carry):
            a = part[place(row, i), :].reshape(T // 8, 8, T)
            a = jnp.round(a * scale).reshape(T, T)
            msg[rows_of(i * T, T), :] = a.astype(jnp.int32).astype(jnp.int16)
            return carry

        lax.fori_loop(0, tiles_in, one, 0)


    planes = {}

    def plane_start(hop):
        own = panel.at[hop, z, x, y]
        for k, (dy, dx) in enumerate(y_plane):
            planes[hop, -dy % NY, dx] = remote(own, own, in_y(dy, dx))
            planes[hop, -dy % NY, dx].start()

    def plane_wait(hop, dx):
        for d in range(1 - dx, NY):
            slot = panel.at[hop, z, 1 - x if dx else x, rem(y + d, NY)]
            landed(slot, planes[hop, d, dx])

    rings = {}

    def ring(hop, i, s):
        if s > 1:
            for copy in rings[hop, i, s - 1]:
                copy.wait_recv()
        xx = 1 - x if i else x
        up, down = panel.at[hop, rem(z - (s - 1), NZ), xx], panel.at[hop, rem(z + (s - 1), NZ), xx]
        pairs = [(up, zp), (down, zm)]
        if s == NZ // 2:
            pairs = pairs[i:i + 1]
        rings[hop, i, s] = [remote(block, block, peer) for block, peer in pairs]
        for copy in rings[hop, i, s]:
            copy.start()

    def ring_products(hop, i, s):
        xx = 1 - x if i else x
        groups = [rem(z - s, NZ) * 2 + xx, rem(z + s, NZ) * 2 + xx]
        each(product_forward, hop, groups if 0 < s < NZ // 2 else groups[:1])

    forward = {}

    def forward_core(hop):
        for i in range(2):
            fsend1[hop, i] = acc[rows_of((2 * i + 1 - core) * T, T), :]
        forward["core", hop] = remote(fsend1.at[hop], frecv1.at[hop], c_core)
        forward["core", hop].start()

    def forward_far(hop):
        forward["core", hop].wait_recv()
        fsend2[hop] = acc[rows_of((2 * (1 - xh) + core) * T, T), :] + frecv1[hop, 1 - xh]
        forward["far", hop] = remote(fsend2.at[hop], frecv2.at[hop], c_xh)
        forward["far", hop].start()

    def forward_end(hop):
        mine = acc[rows_of((2 * xh + core) * T, T), :] + frecv1[hop, xh]
        t_col = jnp.transpose(jnp.broadcast_to(t_row, (T, T)))
        forward["far", hop].wait_recv()
        mine = (1.0 - t_col) * (mine + frecv2[hop]) + t_col * h[...]
        if hop == 0:
            panel[1, z, x, y] = mine.astype(jnp.bfloat16)
        else:
            prop[...] = mine


    queries = {}

    def query_start(hop):
        queries[hop] = [remote(qcat.at[hop, :, lane], qcat.at[hop, :, lane], peer) for peer in (c_far, c_xh, c_core)]
        for copy in queries[hop]:
            copy.start()

    def query_wait(hop):
        for copy in queries[hop]:
            copy.wait_recv()

    reduces = {}

    def pair(j):
        return 2 * rem(zpair + j, 4)

    def reduce_one(hop, j):
        zz = pair(j)
        each(product_adjoint, hop, [zz * 2 + i for i in range(4)])
        for way, peer in ((0, ym), (1, yp)):
            msg = s_one.at[hop, j, way]
            pack_message(msg, tile_row(2, zz, way), 2)
            copy = remote(msg, r_one.at[hop, j, way], peer)
            copy.start()
            reduces[1, hop, j, way] = copy

    def reduce_two(hop, j):
        zz = pair(j)
        for way, peer, dy in ((0, ym, -1), (1, yp, 1)):
            reduces[1, hop, j, way].wait_recv()
            add_message(r_one.at[hop, j, way], tile_row(dy, zz, way), 2)
            msg = s_two.at[hop, j, way]
            pack_message(msg, tile_row(dy, zz, 0), 4)
            copy = remote(msg, r_two.at[hop, j, way], peer)
            copy.start()
            reduces[2, hop, j, way] = copy

    def reduce_x(hop, j):
        zz = pair(j)
        for way in range(2):
            reduces[2, hop, j, way].wait_recv()
            add_message(r_two.at[hop, j, way], tile_row(0, zz, 0), 4)
        msg = s_x.at[hop, j]
        pack_message(msg, tile_row(0, zz, 1 - x), 2)
        reduces[3, hop, j] = remote(msg, r_x.at[hop, j], at(z, y, 1 - x))
        reduces[3, hop, j].start()

    def own_copy(hop, j, i):
        zz = pair(j) + i
        slot = rem(z - zz, NZ)
        copy = pltpu.make_async_remote_copy(
            src_ref=s_own.at[hop, j, i], dst_ref=r_own.at[hop, slot],
            send_sem=so.at[hop, 2 * j + i], recv_sem=ro.at[hop, slot],
            device_id=at(zz, y, x), device_id_type=MESH,
        )
        return copy, slot

    def reduce_own(hop, j):
        zz = pair(j)
        reduces[3, hop, j].wait_recv()
        add_message(r_x.at[hop, j], tile_row(0, zz, x), 2)
        for i in range(2):
            pack_message(s_own.at[hop, j, i], tile_row(0, zz + i, x), 1)
            copy, slot = own_copy(hop, j, i)
            if j:
                copy.start()
            else:
                pl.when(slot != 0)(copy.start)

    def own_done(hop):
        for j in range(4):
            for i in range(2):
                copy, slot = own_copy(hop, j, i)
                if j:
                    copy.wait_send()
                else:
                    pl.when(slot != 0)(copy.wait_send)

    def adjoint_end(hop):
        for slot in range(1, NZ):
            pltpu.make_async_remote_copy(
                src_ref=r_own.at[hop, slot], dst_ref=r_own.at[hop, slot], send_sem=so.at[hop, 0],
                recv_sem=ro.at[hop, slot], device_id=yp, device_id_type=MESH,
            ).wait_recv()

        row = tile_row(0, z, x)

        def one(slot, carry):
            add_message(r_own.at[hop, slot], row, 1)
            return carry

        lax.fori_loop(1, NZ, one, 0)
        d = part[rows_of(row, T), :]
        if hop == 0:
            d_one[...] = d
            qcat[1, :, lane] = (keep_row * d).astype(jnp.bfloat16)
        else:
            grad[...] = jnp.transpose(t_row * jnp.transpose(cot[...]) + t_row * d_one[...] + d)

    pl.semaphore_wait(barrier, len(peers))
    plane_start(0)
    query_start(0)
    load.wait()
    tv[SLOTS] = jnp.zeros((T, T), jnp.bfloat16)

    def fill(g, carry):
        for q in range(COLS):
            for i in range(4):
                ad[g, q * T:(q + 1) * T, i * T:(i + 1) * T] = tv[inv[q * 64 + g * 4 + i]]
        return carry

    lax.fori_loop(0, GROUPS, fill, 0)

    p = PARTS
    query_wait(0)
    acc[...] = jnp.zeros_like(acc)
    for hop in range(2):
        plane_wait(hop, 0)
        ring(hop, 0, 1)
        plane_wait(hop, 1)
        ring(hop, 1, 1)
        if hop == 0:
            reduce_one(hop, p[0])
            reduce_one(hop, p[1])
        ring_products(hop, 0, 0)
        ring(hop, 0, 2)
        if hop == 0:
            reduce_one(hop, p[2])
            reduce_one(hop, p[3])
        ring(hop, 1, 2)
        reduce_two(hop, p[0])
        reduce_two(hop, p[1])
        ring_products(hop, 1, 0)
        ring_products(hop, 0, 1)
        ring_products(hop, 1, 1)
        ring(hop, 0, 3)
        reduce_two(hop, p[2])
        ring(hop, 1, 3)
        reduce_x(hop, p[0])
        reduce_two(hop, p[3])
        ring_products(hop, 0, 2)
        ring_products(hop, 1, 2)
        reduce_x(hop, p[1])
        ring(hop, 0, 4)
        reduce_own(hop, p[0])
        ring(hop, 1, 4)
        reduce_x(hop, p[2])
        reduce_own(hop, p[1])
        ring_products(hop, 0, 3)
        ring_products(hop, 1, 3)
        reduce_x(hop, p[3])
        reduce_own(hop, p[2])
        for i in range(2):
            rings[hop, i, 4][0].wait_recv()
            ring_products(hop, i, 4)
        forward_core(hop)
        reduce_own(hop, p[3])
        forward_far(hop)
        adjoint_end(hop)
        if hop == 0:
            query_start(1)
        forward_end(hop)
        if hop == 0:
            plane_start(1)
            acc[...] = jnp.zeros_like(acc)
            query_wait(1)
            for j in p:
                reduce_one(1, j)

    for copy in sent:
        copy.wait_send()
    for hop in range(2):
        own_done(hop)


def shards(h_start, cotangent, node_type, teleport, tile_values, tile_row, tile_col, tile_count):
    k = tile_col[0, 0]
    place = tile_row[0, 0] * 64 + (k // 8 * 2 + k % 2) * 4 + (k // 2) % 4
    slot = jnp.arange(SLOTS, dtype=jnp.int32)
    place = jnp.where(slot < tile_count[0, 0], place, -1)
    hit = place[None, :] == jnp.arange(COLS * 64, dtype=jnp.int32)[:, None]
    inv = SLOTS + jnp.sum(jnp.where(hit, slot[None, :] - SLOTS, 0), axis=1)

    vmem = pl.BlockSpec(memory_space=pltpu.VMEM)
    smem = pl.BlockSpec(memory_space=pltpu.SMEM)
    tile = jax.ShapeDtypeStruct((T, T), jnp.float32)
    copies = 96
    return pl.pallas_call(
        kernel,
        out_shape=(tile, tile),
        in_specs=[smem, smem, pl.BlockSpec(memory_space=pl.ANY)] + [vmem] * 3,
        out_specs=(vmem, vmem),
        scratch_shapes=[
            pltpu.VMEM((SLOTS + 1, T, T), jnp.bfloat16),
            pltpu.VMEM((GROUPS, 512, 512), jnp.bfloat16),
            pltpu.VMEM((2, NZ, NX, NY, T, T), jnp.bfloat16),
            pltpu.VMEM((64 * T, T), jnp.float32),
            pltpu.VMEM((2, T, COLS * T), jnp.bfloat16),
            pltpu.VMEM((COLS * T, T), jnp.float32),
            pltpu.VMEM((2, 2, T, T), jnp.float32),
            pltpu.VMEM((2, 2, T, T), jnp.float32),
            pltpu.VMEM((2, T, T), jnp.float32),
            pltpu.VMEM((2, T, T), jnp.float32),
            pltpu.VMEM((2, 4, 2, 2 * T + PAD, T), jnp.int16),
            pltpu.VMEM((2, 4, 2, 2 * T + PAD, T), jnp.int16),
            pltpu.VMEM((2, 4, 2, 4 * T + PAD, T), jnp.int16),
            pltpu.VMEM((2, 4, 2, 4 * T + PAD, T), jnp.int16),
            pltpu.VMEM((2, 4, 2 * T + PAD, T), jnp.int16),
            pltpu.VMEM((2, 4, 2 * T + PAD, T), jnp.int16),
            pltpu.VMEM((2, 4, 2, T + PAD, T), jnp.int16),
            pltpu.VMEM((2, NZ, T + PAD, T), jnp.int16),
            pltpu.VMEM((T, T), jnp.float32),
            pltpu.SemaphoreType.DMA,
            pltpu.SemaphoreType.DMA((copies,)),
            pltpu.SemaphoreType.DMA((copies,)),
            pltpu.SemaphoreType.DMA((2, NZ)),
            pltpu.SemaphoreType.DMA((2, NZ)),
        ],
        compiler_params=pltpu.CompilerParams(
            collective_id=0, has_side_effects=True, vmem_limit_bytes=56 << 20
        ),
    )(inv, teleport, tile_values[0, 0], h_start, cotangent, node_type[None, :])


def solution(mesh):
    placed = (
        P(("rows", "cols"), None),
        P(("rows", "cols"), None),
        P(("rows", "cols")),
        P(),
        P("rows", "cols", None, None, None),
        P("rows", "cols", None),
        P("rows", "cols", None),
        P("rows", "cols"),
    )
    return jax.shard_map(
        shards,
        mesh=mesh,
        in_specs=placed,
        out_specs=(P(("rows", "cols"), None), P(("rows", "cols"), None)),
        check_vma=False,
    )
```

```python
import jax
import jax.numpy as jnp
from jax import lax
from jax.experimental import pallas as pl
from jax.experimental.pallas import tpu as pltpu
from jax.sharding import PartitionSpec as P

MESH = pl.DeviceIdType.MESH
T = 128
NZ, NY, NX = 8, 4, 2
COLS = 4
GROUPS = 16
SLOTS = 192
PAD = 16
PARTS = (2, 1, 3, 0)


def rem(a, n):
    return lax.rem(a + 2 * n, n)


def kernel(
    inv, rates, tiles, h, cot, types, prop, grad,
    tv, ad, panel, part, qcat, acc, s_cols, r_cols,
    s_one, r_one, s_two, r_two, s_x, r_x, s_own, r_own, d_one,
    load_sem, ssem, rsem, so, ro,
):
    r = lax.axis_index("rows")
    c = lax.axis_index("cols")
    z, y, x = r // 8, lax.rem(r // 2, 4), lax.rem(r, 2)
    xh, core = c // 2, lax.rem(c, 2)
    zpair = z // 2

    def at(zz, yy, xx):
        return {"rows": zz * 8 + yy * 2 + xx, "cols": c}

    zp, zm = at(rem(z + 1, NZ), y, x), at(rem(z - 1, NZ), y, x)
    yp, ym = at(z, rem(y + 1, NY), x), at(z, rem(y - 1, NY), x)
    c_core = {"rows": r, "cols": xh * 2 + 1 - core}
    c_xh = {"rows": r, "cols": (1 - xh) * 2 + core}
    c_far = {"rows": r, "cols": (1 - xh) * 2 + 1 - core}
    y_plane = [(dy, dx) for dy in (2, 1, 3, 0) for dx in (1, 0) if dy or dx]

    def in_y(dy, dx):
        return at(z, rem(y + dy, NY), 1 - x if dx else x)

    load = pltpu.make_async_copy(tiles, tv.at[pl.ds(1, SLOTS)], load_sem)
    load.start()

    barrier = pltpu.get_barrier_semaphore()
    peers = [in_y(*p) for p in y_plane] + [at(rem(z + d, NZ), y, x) for d in range(1, NZ)] + [c_core, c_xh, c_far]
    for peer in peers:
        pl.semaphore_signal(barrier, inc=1, device_id=peer, device_id_type=MESH)

    t_row = jnp.zeros((1, T), jnp.float32)
    for i in range(8):
        t_row = t_row + jnp.where(types[...] == i, rates[i], 0.0)
    keep_row = 1.0 - t_row
    lane = pl.ds(pl.multiple_of(c * T, T), T)
    panel[0, z, x, y] = h[...].astype(jnp.bfloat16)
    qcat[0, :, lane] = (keep_row * jnp.transpose(cot[...])).astype(jnp.bfloat16)

    counter = [0]
    sent = []

    def remote(src, dst, peer):
        k = counter[0]
        counter[0] += 1
        copy = pltpu.make_async_remote_copy(
            src_ref=src, dst_ref=dst, send_sem=ssem.at[k], recv_sem=rsem.at[k],
            device_id=peer, device_id_type=MESH,
        )
        copy.index = k
        sent.append(copy)
        return copy

    def landed(slot, copy):
        pltpu.make_async_remote_copy(
            src_ref=slot, dst_ref=slot, send_sem=ssem.at[copy.index], recv_sem=rsem.at[copy.index],
            device_id=yp, device_id_type=MESH,
        ).wait_recv()

    def rows_of(start, size):
        return pl.ds(pl.multiple_of(start, T), size)

    def each(fn, hop, groups):
        def one(i, carry):
            g = groups[-1]
            for k in range(len(groups) - 1):
                g = jnp.where(i == k, groups[k], g)
            fn(hop, g)
            return carry

        lax.fori_loop(0, len(groups), one, 0)

    def tile_row(dy, zz, xx):
        return (rem(y + dy, NY) * 16 + xx * 8 + zz) * T

    def product_adjoint(hop, g):
        res = jnp.dot(qcat[hop], ad[g], preferred_element_type=jnp.float32)
        for i in range(NY):
            part[rows_of((i * 16 + lax.rem(g, 2) * 8 + g // 2) * T, T), :] = res[:, i * T:(i + 1) * T]

    def product_forward(hop, g):
        tile4 = panel[hop, g // 2, lax.rem(g, 2)].reshape(NY * T, T)
        acc[...] += jnp.dot(ad[g], tile4, preferred_element_type=jnp.float32)

    def decode(msg, row, scale):
        val = msg[rows_of(row, T), :].astype(jnp.int32).astype(jnp.float32)
        return (val.reshape(T // 8, 8, T) * scale).reshape(T, T)

    def scale_of(msg, rows):
        e = msg[pl.ds(rows, PAD), :].astype(jnp.int32).astype(jnp.float32)
        return jnp.exp2(e - 14.0)[None, 0:8, :]

    def place(row, i):
        return rows_of(row + (i // 2) * 8 * T + lax.rem(i, 2) * T, T)

    def add_message(msg, row, tiles_in):
        scale = scale_of(msg, tiles_in * T)

        def one(i, carry):
            where = place(row, i)
            part[where, :] = part[where, :] + decode(msg, i * T, scale)
            return carry

        lax.fori_loop(0, tiles_in, one, 0)

    def pack_message(msg, row, tiles_in):
        def largest(i, m):
            a = jnp.abs(part[place(row, i), :]).reshape(T // 8, 8, T)
            return jnp.maximum(m, jnp.max(a, axis=0))

        m = lax.fori_loop(0, tiles_in, largest, jnp.full((8, T), 1e-30, jnp.float32))
        e = jnp.ceil(jnp.log2(jnp.max(m, axis=0, keepdims=True)))
        scale = jnp.broadcast_to(jnp.exp2(14.0 - e), (8, T))[None]
        msg[pl.ds(tiles_in * T, PAD), :] = jnp.broadcast_to(e, (PAD, T)).astype(jnp.int32).astype(jnp.int16)

        def one(i, carry):
            a = part[place(row, i), :].reshape(T // 8, 8, T)
            a = jnp.round(a * scale).reshape(T, T)
            msg[rows_of(i * T, T), :] = a.astype(jnp.int32).astype(jnp.int16)
            return carry

        lax.fori_loop(0, tiles_in, one, 0)


    planes = {}

    def plane_start(hop):
        own = panel.at[hop, z, x, y]
        for k, (dy, dx) in enumerate(y_plane):
            planes[hop, -dy % NY, dx] = remote(own, own, in_y(dy, dx))
            planes[hop, -dy % NY, dx].start()

    def plane_wait(hop, dx):
        for d in range(1 - dx, NY):
            slot = panel.at[hop, z, 1 - x if dx else x, rem(y + d, NY)]
            landed(slot, planes[hop, d, dx])

    rings, crossed = {}, {}

    def ring(hop, i, s):
        xx = x if i < 2 else 1 - x
        part_of = pl.ds(2 * (i % 2), 2)
        if s > 1:
            for copy in rings[hop, i, s - 1]:
                copy.wait_recv()
        blocks = [rem(z - (s - 1), NZ), rem(z + (s - 1), NZ)]
        up, down = [panel.at[hop, b, xx, part_of] for b in blocks]
        pairs = [(up, zp), (down, zm)]
        if s == NZ // 2:
            half = panel.at[hop, blocks[0], xx, pl.ds(2 * (i % 2), 1)], panel.at[hop, blocks[1], xx, pl.ds(2 * (i % 2) + 1, 1)]
            pairs = [(half[0], zp), (half[1], zm)]
        rings[hop, i, s] = [remote(block, block, peer) for block, peer in pairs]
        for copy in rings[hop, i, s]:
            copy.start()
        if i == 0 and s > 1:
            cross(hop, s - 1)

    def cross(hop, s):
        part_of = pl.ds(0, 2)
        blocks = [rem(z - s, NZ), rem(z + s, NZ)]
        if s == NZ // 2:
            blocks = blocks[:1]
        crossed[hop, s] = [remote(panel.at[hop, b, x, part_of], panel.at[hop, b, x, part_of], at(z, y, 1 - x)) for b in blocks]
        for copy in crossed[hop, s]:
            copy.start()

    def ring_end(hop, i):
        for copy in rings[hop, i, NZ // 2]:
            copy.wait_recv()
        if i == 0:
            cross(hop, NZ // 2)

    def cross_wait(hop, s):
        blocks = [rem(z - s, NZ), rem(z + s, NZ)]
        for b, copy in zip(blocks, crossed[hop, s]):
            landed(panel.at[hop, b, 1 - x, pl.ds(0, 2)], copy)

    def ring_products(hop, i, s):
        xx = 1 - x if i else x
        groups = [rem(z - s, NZ) * 2 + xx, rem(z + s, NZ) * 2 + xx]
        each(product_forward, hop, groups if 0 < s < NZ // 2 else groups[:1])

    forward = {}

    def pack_tile(msg, a):
        m = jnp.max(jnp.abs(a).reshape(T // 8, 8, T), axis=0)
        e = jnp.ceil(jnp.log2(jnp.maximum(jnp.max(m, axis=0, keepdims=True), 1e-30)))
        msg[pl.ds(T, PAD), :] = jnp.broadcast_to(e, (PAD, T)).astype(jnp.int32).astype(jnp.int16)
        scale = jnp.broadcast_to(jnp.exp2(14.0 - e), (8, T))[None]
        a = jnp.round(a.reshape(T // 8, 8, T) * scale).reshape(T, T)
        msg[pl.ds(0, T), :] = a.astype(jnp.int32).astype(jnp.int16)

    def forward_send(hop):
        targets = ((c_far, (1 - xh) * 2 + 1 - core), (c_xh, (1 - xh) * 2 + core), (c_core, xh * 2 + 1 - core))
        forward[hop] = []
        for k, (peer, q) in enumerate(targets):
            pack_tile(s_cols.at[hop, k], acc[rows_of(q * T, T), :])
            copy = remote(s_cols.at[hop, k], r_cols.at[hop, k], peer)
            copy.start()
            forward[hop].append(copy)

    def forward_end(hop):
        mine = acc[rows_of(c * T, T), :]
        t_col = jnp.transpose(jnp.broadcast_to(t_row, (T, T)))
        for k in (2, 1, 0):
            forward[hop][k].wait_recv()
            msg = r_cols.at[hop, k]
            mine = mine + decode(msg, 0, scale_of(msg, T))
        mine = (1.0 - t_col) * mine + t_col * h[...]
        if hop == 0:
            panel[1, z, x, y] = mine.astype(jnp.bfloat16)
        else:
            prop[...] = mine


    queries = {}

    def query_start(hop):
        queries[hop] = [remote(qcat.at[hop, :, lane], qcat.at[hop, :, lane], peer) for peer in (c_far, c_xh, c_core)]
        for copy in queries[hop]:
            copy.start()

    def query_wait(hop):
        for copy in queries[hop]:
            copy.wait_recv()

    reduces = {}

    def pair(j):
        return 2 * rem(zpair + j, 4)

    def reduce_one(hop, j):
        zz = pair(j)
        each(product_adjoint, hop, [zz * 2 + i for i in range(4)])
        for way, peer in ((0, ym), (1, yp)):
            msg = s_one.at[hop, j, way]
            pack_message(msg, tile_row(2, zz, way), 2)
            copy = remote(msg, r_one.at[hop, j, way], peer)
            copy.start()
            reduces[1, hop, j, way] = copy

    def reduce_two(hop, j):
        zz = pair(j)
        for way, peer, dy in ((0, ym, -1), (1, yp, 1)):
            reduces[1, hop, j, way].wait_recv()
            add_message(r_one.at[hop, j, way], tile_row(dy, zz, way), 2)
            msg = s_two.at[hop, j, way]
            pack_message(msg, tile_row(dy, zz, 0), 4)
            copy = remote(msg, r_two.at[hop, j, way], peer)
            copy.start()
            reduces[2, hop, j, way] = copy

    def reduce_x(hop, j):
        zz = pair(j)
        for way in range(2):
            reduces[2, hop, j, way].wait_recv()
            add_message(r_two.at[hop, j, way], tile_row(0, zz, 0), 4)
        msg = s_x.at[hop, j]
        pack_message(msg, tile_row(0, zz, 1 - x), 2)
        reduces[3, hop, j] = remote(msg, r_x.at[hop, j], at(z, y, 1 - x))
        reduces[3, hop, j].start()

    def own_copy(hop, j, i):
        zz = pair(j) + i
        slot = rem(z - zz, NZ)
        copy = pltpu.make_async_remote_copy(
            src_ref=s_own.at[hop, j, i], dst_ref=r_own.at[hop, slot],
            send_sem=so.at[hop, 2 * j + i], recv_sem=ro.at[hop, slot],
            device_id=at(zz, y, x), device_id_type=MESH,
        )
        return copy, slot

    def reduce_own(hop, j):
        zz = pair(j)
        reduces[3, hop, j].wait_recv()
        add_message(r_x.at[hop, j], tile_row(0, zz, x), 2)
        for i in range(2):
            pack_message(s_own.at[hop, j, i], tile_row(0, zz + i, x), 1)
            copy, slot = own_copy(hop, j, i)
            if j:
                copy.start()
            else:
                pl.when(slot != 0)(copy.start)

    def own_done(hop):
        for j in range(4):
            for i in range(2):
                copy, slot = own_copy(hop, j, i)
                if j:
                    copy.wait_send()
                else:
                    pl.when(slot != 0)(copy.wait_send)

    def adjoint_end(hop):
        for slot in range(1, NZ):
            pltpu.make_async_remote_copy(
                src_ref=r_own.at[hop, slot], dst_ref=r_own.at[hop, slot], send_sem=so.at[hop, 0],
                recv_sem=ro.at[hop, slot], device_id=yp, device_id_type=MESH,
            ).wait_recv()

        row = tile_row(0, z, x)

        def one(slot, carry):
            add_message(r_own.at[hop, slot], row, 1)
            return carry

        lax.fori_loop(1, NZ, one, 0)
        d = part[rows_of(row, T), :]
        if hop == 0:
            d_one[...] = d
            qcat[1, :, lane] = (keep_row * d).astype(jnp.bfloat16)
        else:
            grad[...] = jnp.transpose(t_row * jnp.transpose(cot[...]) + t_row * d_one[...] + d)

    pl.semaphore_wait(barrier, len(peers))
    plane_start(0)
    query_start(0)
    load.wait()
    tv[0] = jnp.zeros((T, T), jnp.bfloat16)

    def fill(g, carry):
        for q in range(COLS):
            for i in range(4):
                ad[g, q * T:(q + 1) * T, i * T:(i + 1) * T] = tv[inv[q * 64 + g * 4 + i]]
        return carry

    lax.fori_loop(0, GROUPS, fill, 0)

    p = PARTS
    acc[...] = jnp.zeros_like(acc)

    def ring_begin(hop):
        plane_wait(hop, 0)
        ring(hop, 0, 1)
        ring(hop, 1, 1)
        plane_wait(hop, 1)
        ring(hop, 3, 1)

    ring_begin(0)
    query_wait(0)
    for hop in range(2):
        if hop == 0:
            reduce_one(hop, p[0])
            reduce_one(hop, p[1])
        ring_products(hop, 0, 0)
        ring(hop, 0, 2)
        ring(hop, 1, 2)
        if hop == 0:
            reduce_one(hop, p[2])
            reduce_one(hop, p[3])
        ring(hop, 3, 2)
        reduce_two(hop, p[0])
        reduce_two(hop, p[1])
        ring(hop, 0, 3)
        ring(hop, 1, 3)
        ring_products(hop, 1, 0)
        ring_products(hop, 0, 1)
        ring(hop, 3, 3)
        reduce_two(hop, p[2])
        reduce_x(hop, p[0])
        ring(hop, 0, 4)
        ring(hop, 1, 4)
        reduce_two(hop, p[3])
        cross_wait(hop, 1)
        ring_products(hop, 1, 1)
        ring_products(hop, 0, 2)
        ring(hop, 3, 4)
        reduce_x(hop, p[1])
        reduce_own(hop, p[0])
        cross_wait(hop, 2)
        ring_products(hop, 1, 2)
        ring_products(hop, 0, 3)
        ring_end(hop, 0)
        reduce_x(hop, p[2])
        reduce_own(hop, p[1])
        ring_end(hop, 1)
        cross_wait(hop, 3)
        ring_products(hop, 1, 3)
        ring_products(hop, 0, 4)
        reduce_x(hop, p[3])
        reduce_own(hop, p[2])
        ring_end(hop, 3)
        cross_wait(hop, 4)
        ring_products(hop, 1, 4)
        forward_send(hop)
        reduce_own(hop, p[3])
        forward_end(hop)
        if hop == 0:
            plane_start(1)
            acc[...] = jnp.zeros_like(acc)
        adjoint_end(hop)
        if hop == 0:
            query_start(1)
            ring_begin(1)
            query_wait(1)
            for j in p:
                reduce_one(1, j)

    for copy in sent:
        copy.wait_send()
    for hop in range(2):
        own_done(hop)


def shards(h_start, cotangent, node_type, teleport, tile_values, tile_row, tile_col, tile_count):
    spot = jnp.arange(COLS * 64, dtype=jnp.int32)[:, None]
    row, col = spot // 64, spot % 64 // 8 * 8 + spot % 4 * 2 + spot // 4 % 2
    slot = jnp.arange(SLOTS, dtype=jnp.int32)[None, :]
    hit = (tile_row[0] == row) & (tile_col[0] == col) & (slot < tile_count)
    inv = jnp.sum(jnp.where(hit, slot + 1, 0), axis=1)

    vmem = pl.BlockSpec(memory_space=pltpu.VMEM)
    smem = pl.BlockSpec(memory_space=pltpu.SMEM)
    tile = jax.ShapeDtypeStruct((T, T), jnp.float32)
    copies = 160
    return pl.pallas_call(
        kernel,
        out_shape=(tile, tile),
        in_specs=[smem, smem, pl.BlockSpec(memory_space=pl.ANY)] + [vmem] * 3,
        out_specs=(vmem, vmem),
        scratch_shapes=[
            pltpu.VMEM((SLOTS + 1, T, T), jnp.bfloat16),
            pltpu.VMEM((GROUPS, 512, 512), jnp.bfloat16),
            pltpu.VMEM((2, NZ, NX, NY, T, T), jnp.bfloat16),
            pltpu.VMEM((64 * T, T), jnp.float32),
            pltpu.VMEM((2, T, COLS * T), jnp.bfloat16),
            pltpu.VMEM((COLS * T, T), jnp.float32),
            pltpu.VMEM((2, 3, T + PAD, T), jnp.int16),
            pltpu.VMEM((2, 3, T + PAD, T), jnp.int16),
            pltpu.VMEM((2, 4, 2, 2 * T + PAD, T), jnp.int16),
            pltpu.VMEM((2, 4, 2, 2 * T + PAD, T), jnp.int16),
            pltpu.VMEM((2, 4, 2, 4 * T + PAD, T), jnp.int16),
            pltpu.VMEM((2, 4, 2, 4 * T + PAD, T), jnp.int16),
            pltpu.VMEM((2, 4, 2 * T + PAD, T), jnp.int16),
            pltpu.VMEM((2, 4, 2 * T + PAD, T), jnp.int16),
            pltpu.VMEM((2, 4, 2, T + PAD, T), jnp.int16),
            pltpu.VMEM((2, NZ, T + PAD, T), jnp.int16),
            pltpu.VMEM((T, T), jnp.float32),
            pltpu.SemaphoreType.DMA,
            pltpu.SemaphoreType.DMA((copies,)),
            pltpu.SemaphoreType.DMA((copies,)),
            pltpu.SemaphoreType.DMA((2, NZ)),
            pltpu.SemaphoreType.DMA((2, NZ)),
        ],
        compiler_params=pltpu.CompilerParams(
            collective_id=0, has_side_effects=True, vmem_limit_bytes=56 << 20
        ),
    )(inv, teleport, tile_values[0, 0], h_start, cotangent, node_type[None, :])


def solution(mesh):
    placed = (
        P(("rows", "cols"), None),
        P(("rows", "cols"), None),
        P(("rows", "cols")),
        P(),
        P("rows", "cols", None, None, None),
        P("rows", "cols", None),
        P("rows", "cols", None),
        P("rows", "cols"),
    )
    return jax.shard_map(
        shards,
        mesh=mesh,
        in_specs=placed,
        out_specs=(P(("rows", "cols"), None), P(("rows", "cols"), None)),
        check_vma=False,
    )
```

```python
import jax
import jax.numpy as jnp
from jax import lax
from jax.experimental import pallas as pl
from jax.experimental.pallas import tpu as pltpu
from jax.sharding import PartitionSpec as P

MESH = pl.DeviceIdType.MESH
T = 128
NZ, NY, NX = 8, 4, 2
COLS = 4
GROUPS = 16
SLOTS = 192
PAD = 16
PARTS = (2, 1, 3, 0)


def rem(a, n):
    return lax.rem(a + 2 * n, n)


def kernel(
    inv, rates, tiles, h, cot, types, prop, grad,
    tv, ad, panel, part, qcat, acc, s_cols, r_cols,
    s_one, r_one, s_two, r_two, s_x, r_x, s_own, r_own, d_one,
    load_sem, ssem, rsem, so, ro,
):
    r = lax.axis_index("rows")
    c = lax.axis_index("cols")
    z, y, x = r // 8, lax.rem(r // 2, 4), lax.rem(r, 2)
    xh, core = c // 2, lax.rem(c, 2)
    zpair = z // 2

    def at(zz, yy, xx):
        return {"rows": zz * 8 + yy * 2 + xx, "cols": c}

    zp, zm = at(rem(z + 1, NZ), y, x), at(rem(z - 1, NZ), y, x)
    yp, ym = at(z, rem(y + 1, NY), x), at(z, rem(y - 1, NY), x)
    c_core = {"rows": r, "cols": xh * 2 + 1 - core}
    c_xh = {"rows": r, "cols": (1 - xh) * 2 + core}
    c_far = {"rows": r, "cols": (1 - xh) * 2 + 1 - core}
    y_plane = [(dy, dx) for dy in (2, 1, 3, 0) for dx in (1, 0) if dy or dx]

    def in_y(dy, dx):
        return at(z, rem(y + dy, NY), 1 - x if dx else x)

    load = pltpu.make_async_copy(tiles, tv.at[pl.ds(1, SLOTS)], load_sem)
    load.start()

    barrier = pltpu.get_barrier_semaphore()
    peers = [in_y(*p) for p in y_plane] + [at(rem(z + d, NZ), y, x) for d in range(1, NZ)] + [c_core, c_xh, c_far]
    for peer in peers:
        pl.semaphore_signal(barrier, inc=1, device_id=peer, device_id_type=MESH)

    t_row = jnp.zeros((1, T), jnp.float32)
    for i in range(8):
        t_row = t_row + jnp.where(types[...] == i, rates[i], 0.0)
    keep_row = 1.0 - t_row
    lane = pl.ds(pl.multiple_of(c * T, T), T)
    panel[0, z, x, y] = h[...].astype(jnp.bfloat16)
    qcat[0, :, lane] = (keep_row * jnp.transpose(cot[...])).astype(jnp.bfloat16)

    counter = [0]
    sent = []

    def remote(src, dst, peer):
        k = counter[0]
        counter[0] += 1
        copy = pltpu.make_async_remote_copy(
            src_ref=src, dst_ref=dst, send_sem=ssem.at[k], recv_sem=rsem.at[k],
            device_id=peer, device_id_type=MESH,
        )
        copy.index = k
        sent.append(copy)
        return copy

    def landed(slot, copy):
        pltpu.make_async_remote_copy(
            src_ref=slot, dst_ref=slot, send_sem=ssem.at[copy.index], recv_sem=rsem.at[copy.index],
            device_id=yp, device_id_type=MESH,
        ).wait_recv()

    def rows_of(start, size):
        return pl.ds(pl.multiple_of(start, T), size)

    def each(fn, hop, groups):
        def one(i, carry):
            g = groups[-1]
            for k in range(len(groups) - 1):
                g = jnp.where(i == k, groups[k], g)
            fn(hop, g)
            return carry

        lax.fori_loop(0, len(groups), one, 0)

    def tile_row(dy, zz, xx):
        return (rem(y + dy, NY) * 16 + xx * 8 + zz) * T

    def product_adjoint(hop, g):
        res = jnp.dot(qcat[hop], ad[g], preferred_element_type=jnp.float32)
        for i in range(NY):
            part[rows_of((i * 16 + lax.rem(g, 2) * 8 + g // 2) * T, T), :] = res[:, i * T:(i + 1) * T]

    def product_forward(hop, g):
        tile4 = panel[hop, g // 2, lax.rem(g, 2)].reshape(NY * T, T)
        acc[...] += jnp.dot(ad[g], tile4, preferred_element_type=jnp.float32)

    def decode(msg, row, scale):
        val = msg[rows_of(row, T), :].astype(jnp.int32).astype(jnp.float32)
        return (val.reshape(T // 8, 8, T) * scale).reshape(T, T)

    def scale_of(msg, rows):
        e = msg[pl.ds(rows, PAD), :].astype(jnp.int32).astype(jnp.float32)
        return jnp.exp2(e - 14.0)[None, 0:8, :]

    def place(row, i):
        return rows_of(row + (i // 2) * 8 * T + lax.rem(i, 2) * T, T)

    def add_message(msg, row, tiles_in):
        scale = scale_of(msg, tiles_in * T)

        def one(i, carry):
            where = place(row, i)
            part[where, :] = part[where, :] + decode(msg, i * T, scale)
            return carry

        lax.fori_loop(0, tiles_in, one, 0)

    def pack_message(msg, row, tiles_in):
        def largest(i, m):
            a = jnp.abs(part[place(row, i), :]).reshape(T // 8, 8, T)
            return jnp.maximum(m, jnp.max(a, axis=0))

        m = lax.fori_loop(0, tiles_in, largest, jnp.full((8, T), 1e-30, jnp.float32))
        e = jnp.ceil(jnp.log2(jnp.max(m, axis=0, keepdims=True)))
        scale = jnp.broadcast_to(jnp.exp2(14.0 - e), (8, T))[None]
        msg[pl.ds(tiles_in * T, PAD), :] = jnp.broadcast_to(e, (PAD, T)).astype(jnp.int32).astype(jnp.int16)

        def one(i, carry):
            a = part[place(row, i), :].reshape(T // 8, 8, T)
            a = jnp.round(a * scale).reshape(T, T)
            msg[rows_of(i * T, T), :] = a.astype(jnp.int32).astype(jnp.int16)
            return carry

        lax.fori_loop(0, tiles_in, one, 0)


    planes = {}

    def plane_start(hop):
        own = panel.at[hop, z, x, y]
        for k, (dy, dx) in enumerate(y_plane):
            planes[hop, -dy % NY, dx] = remote(own, own, in_y(dy, dx))
            planes[hop, -dy % NY, dx].start()

    def plane_wait(hop, dx):
        for d in range(1 - dx, NY):
            slot = panel.at[hop, z, 1 - x if dx else x, rem(y + d, NY)]
            landed(slot, planes[hop, d, dx])

    rings, crossed = {}, {}

    def ring(hop, i, s):
        xx = x if i < 2 else 1 - x
        part_of = pl.ds(2 * (i % 2), 2)
        if s > 1:
            for copy in rings[hop, i, s - 1]:
                copy.wait_recv()
        blocks = [rem(z - (s - 1), NZ), rem(z + (s - 1), NZ)]
        up, down = [panel.at[hop, b, xx, part_of] for b in blocks]
        pairs = [(up, zp), (down, zm)]
        if s == NZ // 2:
            half = panel.at[hop, blocks[0], xx, pl.ds(2 * (i % 2), 1)], panel.at[hop, blocks[1], xx, pl.ds(2 * (i % 2) + 1, 1)]
            pairs = [(half[0], zp), (half[1], zm)]
        rings[hop, i, s] = [remote(block, block, peer) for block, peer in pairs]
        for copy in rings[hop, i, s]:
            copy.start()
        if i == 0 and s > 1:
            cross(hop, s - 1)

    def cross(hop, s):
        part_of = pl.ds(0, 2)
        blocks = [rem(z - s, NZ), rem(z + s, NZ)]
        if s == NZ // 2:
            blocks = blocks[:1]
        crossed[hop, s] = [remote(panel.at[hop, b, x, part_of], panel.at[hop, b, x, part_of], at(z, y, 1 - x)) for b in blocks]
        for copy in crossed[hop, s]:
            copy.start()

    def ring_end(hop, i):
        for copy in rings[hop, i, NZ // 2]:
            copy.wait_recv()
        if i == 0:
            cross(hop, NZ // 2)

    def cross_wait(hop, s):
        blocks = [rem(z - s, NZ), rem(z + s, NZ)]
        for b, copy in zip(blocks, crossed[hop, s]):
            landed(panel.at[hop, b, 1 - x, pl.ds(0, 2)], copy)

    def ring_products(hop, i, s):
        xx = 1 - x if i else x
        groups = [rem(z - s, NZ) * 2 + xx, rem(z + s, NZ) * 2 + xx]
        each(product_forward, hop, groups if 0 < s < NZ // 2 else groups[:1])

    forward = {}

    def pack_tile(msg, a):
        m = jnp.max(jnp.abs(a).reshape(T // 8, 8, T), axis=0)
        e = jnp.ceil(jnp.log2(jnp.maximum(jnp.max(m, axis=0, keepdims=True), 1e-30)))
        msg[pl.ds(T, PAD), :] = jnp.broadcast_to(e, (PAD, T)).astype(jnp.int32).astype(jnp.int16)
        scale = jnp.broadcast_to(jnp.exp2(14.0 - e), (8, T))[None]
        a = jnp.round(a.reshape(T // 8, 8, T) * scale).reshape(T, T)
        msg[pl.ds(0, T), :] = a.astype(jnp.int32).astype(jnp.int16)

    def forward_send(hop):
        targets = ((c_far, (1 - xh) * 2 + 1 - core), (c_xh, (1 - xh) * 2 + core), (c_core, xh * 2 + 1 - core))
        forward[hop] = []
        for k, (peer, q) in enumerate(targets):
            pack_tile(s_cols.at[hop, k], acc[rows_of(q * T, T), :])
            copy = remote(s_cols.at[hop, k], r_cols.at[hop, k], peer)
            copy.start()
            forward[hop].append(copy)

    def forward_end(hop):
        mine = acc[rows_of(c * T, T), :]
        t_col = jnp.transpose(jnp.broadcast_to(t_row, (T, T)))
        for k in (2, 1, 0):
            forward[hop][k].wait_recv()
            msg = r_cols.at[hop, k]
            mine = mine + decode(msg, 0, scale_of(msg, T))
        mine = (1.0 - t_col) * mine + t_col * h[...]
        if hop == 0:
            panel[1, z, x, y] = mine.astype(jnp.bfloat16)
        else:
            prop[...] = mine


    queries = {}

    def query_start(hop):
        queries[hop] = [remote(qcat.at[hop, :, lane], qcat.at[hop, :, lane], peer) for peer in (c_far, c_xh, c_core)]
        for copy in queries[hop]:
            copy.start()

    def query_wait(hop):
        for copy in queries[hop]:
            copy.wait_recv()

    reduces = {}

    def pair(j):
        return 2 * rem(zpair + j, 4)

    def reduce_one(hop, j):
        zz = pair(j)
        each(product_adjoint, hop, [zz * 2 + i for i in range(4)])
        for way, peer in ((0, ym), (1, yp)):
            msg = s_one.at[hop, j, way]
            pack_message(msg, tile_row(2, zz, way), 2)
            copy = remote(msg, r_one.at[hop, j, way], peer)
            copy.start()
            reduces[1, hop, j, way] = copy

    def reduce_two(hop, j):
        zz = pair(j)
        for way, peer, dy in ((0, ym, -1), (1, yp, 1)):
            reduces[1, hop, j, way].wait_recv()
            add_message(r_one.at[hop, j, way], tile_row(dy, zz, way), 2)
            msg = s_two.at[hop, j, way]
            pack_message(msg, tile_row(dy, zz, 0), 4)
            copy = remote(msg, r_two.at[hop, j, way], peer)
            copy.start()
            reduces[2, hop, j, way] = copy

    def reduce_x(hop, j):
        zz = pair(j)
        for way in range(2):
            reduces[2, hop, j, way].wait_recv()
            add_message(r_two.at[hop, j, way], tile_row(0, zz, 0), 4)
        msg = s_x.at[hop, j]
        pack_message(msg, tile_row(0, zz, 1 - x), 2)
        reduces[3, hop, j] = remote(msg, r_x.at[hop, j], at(z, y, 1 - x))
        reduces[3, hop, j].start()

    def own_copy(hop, j, i):
        zz = pair(j) + i
        slot = rem(z - zz, NZ)
        copy = pltpu.make_async_remote_copy(
            src_ref=s_own.at[hop, j, i], dst_ref=r_own.at[hop, slot],
            send_sem=so.at[hop, 2 * j + i], recv_sem=ro.at[hop, slot],
            device_id=at(zz, y, x), device_id_type=MESH,
        )
        return copy, slot

    def reduce_own(hop, j):
        zz = pair(j)
        reduces[3, hop, j].wait_recv()
        add_message(r_x.at[hop, j], tile_row(0, zz, x), 2)
        for i in range(2):
            pack_message(s_own.at[hop, j, i], tile_row(0, zz + i, x), 1)
            copy, slot = own_copy(hop, j, i)
            if j:
                copy.start()
            else:
                pl.when(slot != 0)(copy.start)

    def own_done(hop):
        for j in range(4):
            for i in range(2):
                copy, slot = own_copy(hop, j, i)
                if j:
                    copy.wait_send()
                else:
                    pl.when(slot != 0)(copy.wait_send)

    def adjoint_end(hop):
        row = tile_row(0, z, x)
        for slot in (4, 3, 5, 2, 6, 7, 1):
            pltpu.make_async_remote_copy(
                src_ref=r_own.at[hop, slot], dst_ref=r_own.at[hop, slot], send_sem=so.at[hop, 0],
                recv_sem=ro.at[hop, slot], device_id=yp, device_id_type=MESH,
            ).wait_recv()
            add_message(r_own.at[hop, slot], row, 1)

        d = part[rows_of(row, T), :]
        if hop == 0:
            d_one[...] = d
            qcat[1, :, lane] = (keep_row * d).astype(jnp.bfloat16)
        else:
            grad[...] = jnp.transpose(t_row * jnp.transpose(cot[...]) + t_row * d_one[...] + d)

    pl.semaphore_wait(barrier, len(peers))
    plane_start(0)
    query_start(0)
    load.wait()
    tv[0] = jnp.zeros((T, T), jnp.bfloat16)

    def fill(g, carry):
        for q in range(COLS):
            for i in range(4):
                ad[g, q * T:(q + 1) * T, i * T:(i + 1) * T] = tv[inv[q * 64 + g * 4 + i]]
        return carry

    lax.fori_loop(0, GROUPS, fill, 0)

    p = PARTS
    acc[...] = jnp.zeros_like(acc)

    def ring_begin(hop):
        plane_wait(hop, 0)
        ring(hop, 0, 1)
        ring(hop, 1, 1)
        plane_wait(hop, 1)
        ring(hop, 3, 1)

    ring_begin(0)
    query_wait(0)
    for hop in range(2):
        if hop == 0:
            reduce_one(hop, p[0])
            reduce_one(hop, p[1])
        ring_products(hop, 0, 0)
        ring(hop, 0, 2)
        ring(hop, 1, 2)
        if hop == 0:
            reduce_one(hop, p[2])
            reduce_one(hop, p[3])
        ring(hop, 3, 2)
        reduce_two(hop, p[0])
        reduce_two(hop, p[1])
        ring(hop, 0, 3)
        ring(hop, 1, 3)
        ring_products(hop, 1, 0)
        ring_products(hop, 0, 1)
        ring(hop, 3, 3)
        reduce_two(hop, p[2])
        reduce_x(hop, p[0])
        ring(hop, 0, 4)
        ring(hop, 1, 4)
        reduce_two(hop, p[3])
        cross_wait(hop, 1)
        ring_products(hop, 1, 1)
        ring_products(hop, 0, 2)
        ring(hop, 3, 4)
        reduce_x(hop, p[1])
        reduce_own(hop, p[0])
        cross_wait(hop, 2)
        ring_products(hop, 1, 2)
        ring_products(hop, 0, 3)
        ring_end(hop, 0)
        reduce_x(hop, p[2])
        reduce_own(hop, p[1])
        ring_end(hop, 1)
        cross_wait(hop, 3)
        ring_products(hop, 1, 3)
        ring_products(hop, 0, 4)
        reduce_x(hop, p[3])
        reduce_own(hop, p[2])
        ring_end(hop, 3)
        cross_wait(hop, 4)
        ring_products(hop, 1, 4)
        forward_send(hop)
        reduce_own(hop, p[3])
        adjoint_end(hop)
        if hop == 0:
            query_start(1)
        forward_end(hop)
        if hop == 0:
            plane_start(1)
            acc[...] = jnp.zeros_like(acc)
            ring_begin(1)
            query_wait(1)
            for j in p:
                reduce_one(1, j)

    for copy in sent:
        copy.wait_send()
    for hop in range(2):
        own_done(hop)


def hand_over(a, b, prop, grad):
    prop[...] = a[...]
    grad[...] = b[...]


def shards(h_start, cotangent, node_type, teleport, tile_values, tile_row, tile_col, tile_count):
    spot = jnp.arange(COLS * 64, dtype=jnp.int32)[:, None]
    row, col = spot // 64, spot % 64 // 8 * 8 + spot % 4 * 2 + spot // 4 % 2
    slot = jnp.arange(SLOTS, dtype=jnp.int32)[None, :]
    hit = (tile_row[0] == row) & (tile_col[0] == col) & (slot < tile_count)
    inv = jnp.sum(jnp.where(hit, slot + 1, 0), axis=1)

    vmem = pl.BlockSpec(memory_space=pltpu.VMEM)
    smem = pl.BlockSpec(memory_space=pltpu.SMEM)
    tile = jax.ShapeDtypeStruct((T, T), jnp.float32)
    copies = 160
    raw = pl.pallas_call(
        kernel,
        out_shape=(tile, tile),
        in_specs=[smem, smem, pl.BlockSpec(memory_space=pl.ANY)] + [vmem] * 3,
        out_specs=(vmem, vmem),
        scratch_shapes=[
            pltpu.VMEM((SLOTS + 1, T, T), jnp.bfloat16),
            pltpu.VMEM((GROUPS, 512, 512), jnp.bfloat16),
            pltpu.VMEM((2, NZ, NX, NY, T, T), jnp.bfloat16),
            pltpu.VMEM((64 * T, T), jnp.float32),
            pltpu.VMEM((2, T, COLS * T), jnp.bfloat16),
            pltpu.VMEM((COLS * T, T), jnp.float32),
            pltpu.VMEM((2, 3, T + PAD, T), jnp.int16),
            pltpu.VMEM((2, 3, T + PAD, T), jnp.int16),
            pltpu.VMEM((2, 4, 2, 2 * T + PAD, T), jnp.int16),
            pltpu.VMEM((2, 4, 2, 2 * T + PAD, T), jnp.int16),
            pltpu.VMEM((2, 4, 2, 4 * T + PAD, T), jnp.int16),
            pltpu.VMEM((2, 4, 2, 4 * T + PAD, T), jnp.int16),
            pltpu.VMEM((2, 4, 2 * T + PAD, T), jnp.int16),
            pltpu.VMEM((2, 4, 2 * T + PAD, T), jnp.int16),
            pltpu.VMEM((2, 4, 2, T + PAD, T), jnp.int16),
            pltpu.VMEM((2, NZ, T + PAD, T), jnp.int16),
            pltpu.VMEM((T, T), jnp.float32),
            pltpu.SemaphoreType.DMA,
            pltpu.SemaphoreType.DMA((copies,)),
            pltpu.SemaphoreType.DMA((copies,)),
            pltpu.SemaphoreType.DMA((2, NZ)),
            pltpu.SemaphoreType.DMA((2, NZ)),
        ],
        compiler_params=pltpu.CompilerParams(
            collective_id=0, has_side_effects=True, vmem_limit_bytes=56 << 20
        ),
    )(inv, teleport, tile_values[0, 0], h_start, cotangent, node_type[None, :])
    return pl.pallas_call(
        hand_over,
        out_shape=(tile, tile),
        in_specs=[vmem, vmem],
        out_specs=(vmem, vmem),
    )(*raw)


def solution(mesh):
    placed = (
        P(("rows", "cols"), None),
        P(("rows", "cols"), None),
        P(("rows", "cols")),
        P(),
        P("rows", "cols", None, None, None),
        P("rows", "cols", None),
        P("rows", "cols", None),
        P("rows", "cols"),
    )
    return jax.shard_map(
        shards,
        mesh=mesh,
        in_specs=placed,
        out_specs=(P(("rows", "cols"), None), P(("rows", "cols"), None)),
        check_vma=False,
    )
```

```python
import jax
import jax.numpy as jnp
from jax import lax
from jax.experimental import pallas as pl
from jax.experimental.pallas import tpu as pltpu
from jax.sharding import PartitionSpec as P

MESH = pl.DeviceIdType.MESH
T = 128
NZ, NY, NX = 8, 4, 2
COLS = 4
GROUPS = 16
SLOTS = 192
PAD = 16
PARTS = (2, 1, 3, 0)


def rem(a, n):
    return lax.rem(a + 2 * n, n)


def kernel(
    inv, rates, tiles, h, cot, types, prop, grad,
    tv, ad, panel, part, qcat, acc, s_cols, r_cols,
    s_one, r_one, s_two, r_two, s_x, r_x, s_own, r_own, d_one,
    load_sem, ssem, rsem, so, ro,
):
    r = lax.axis_index("rows")
    c = lax.axis_index("cols")
    z, y, x = r // 8, lax.rem(r // 2, 4), lax.rem(r, 2)
    xh, core = c // 2, lax.rem(c, 2)
    zpair = z // 2

    def at(zz, yy, xx):
        return {"rows": zz * 8 + yy * 2 + xx, "cols": c}

    zp, zm = at(rem(z + 1, NZ), y, x), at(rem(z - 1, NZ), y, x)
    yp, ym = at(z, rem(y + 1, NY), x), at(z, rem(y - 1, NY), x)
    c_core = {"rows": r, "cols": xh * 2 + 1 - core}
    c_xh = {"rows": r, "cols": (1 - xh) * 2 + core}
    c_far = {"rows": r, "cols": (1 - xh) * 2 + 1 - core}
    y_plane = [(dy, dx) for dy in (2, 1, 3, 0) for dx in (1, 0) if dy or dx]

    def in_y(dy, dx):
        return at(z, rem(y + dy, NY), 1 - x if dx else x)

    load = pltpu.make_async_copy(tiles, tv.at[pl.ds(1, SLOTS)], load_sem)
    load.start()

    barrier = pltpu.get_barrier_semaphore()
    peers = [in_y(*p) for p in y_plane] + [at(rem(z + d, NZ), y, x) for d in range(1, NZ)] + [c_core, c_xh, c_far]
    for peer in peers:
        pl.semaphore_signal(barrier, inc=1, device_id=peer, device_id_type=MESH)

    t_row = jnp.zeros((1, T), jnp.float32)
    for i in range(8):
        t_row = t_row + jnp.where(types[...] == i, rates[i], 0.0)
    keep_row = 1.0 - t_row
    lane = pl.ds(pl.multiple_of(c * T, T), T)
    panel[0, z, x, y] = h[...].astype(jnp.bfloat16)
    qcat[0, :, lane] = (keep_row * jnp.transpose(cot[...])).astype(jnp.bfloat16)

    counter = [0]
    sent = []

    def remote(src, dst, peer):
        k = counter[0]
        counter[0] += 1
        copy = pltpu.make_async_remote_copy(
            src_ref=src, dst_ref=dst, send_sem=ssem.at[k], recv_sem=rsem.at[k],
            device_id=peer, device_id_type=MESH,
        )
        copy.index = k
        sent.append(copy)
        return copy

    def landed(slot, copy):
        pltpu.make_async_remote_copy(
            src_ref=slot, dst_ref=slot, send_sem=ssem.at[copy.index], recv_sem=rsem.at[copy.index],
            device_id=yp, device_id_type=MESH,
        ).wait_recv()

    def rows_of(start, size):
        return pl.ds(pl.multiple_of(start, T), size)

    def each(fn, hop, groups):
        def one(i, carry):
            g = groups[-1]
            for k in range(len(groups) - 1):
                g = jnp.where(i == k, groups[k], g)
            fn(hop, g)
            return carry

        lax.fori_loop(0, len(groups), one, 0)

    def tile_row(dy, zz, xx):
        return (rem(y + dy, NY) * 16 + xx * 8 + zz) * T

    def product_adjoint(hop, g):
        res = jnp.dot(qcat[hop], ad[g], preferred_element_type=jnp.float32)
        for i in range(NY):
            part[rows_of((i * 16 + lax.rem(g, 2) * 8 + g // 2) * T, T), :] = res[:, i * T:(i + 1) * T]

    def product_forward(hop, g):
        tile4 = panel[hop, g // 2, lax.rem(g, 2)].reshape(NY * T, T)
        acc[...] += jnp.dot(ad[g], tile4, preferred_element_type=jnp.float32)

    def decode(msg, row, scale):
        val = msg[rows_of(row, T), :].astype(jnp.int32).astype(jnp.float32)
        return (val.reshape(T // 8, 8, T) * scale).reshape(T, T)

    def scale_of(msg, rows):
        e = msg[pl.ds(rows, PAD), :].astype(jnp.int32).astype(jnp.float32)
        return jnp.exp2(e - 14.0)[None, 0:8, :]

    def place(row, i):
        return rows_of(row + (i // 2) * 8 * T + lax.rem(i, 2) * T, T)

    def add_message(msg, row, tiles_in):
        scale = scale_of(msg, tiles_in * T)

        def one(i, carry):
            where = place(row, i)
            part[where, :] = part[where, :] + decode(msg, i * T, scale)
            return carry

        lax.fori_loop(0, tiles_in, one, 0)

    def pack_message(msg, row, tiles_in):
        def largest(i, m):
            a = jnp.abs(part[place(row, i), :]).reshape(T // 8, 8, T)
            return jnp.maximum(m, jnp.max(a, axis=0))

        m = lax.fori_loop(0, tiles_in, largest, jnp.full((8, T), 1e-30, jnp.float32))
        e = jnp.ceil(jnp.log2(jnp.max(m, axis=0, keepdims=True)))
        scale = jnp.broadcast_to(jnp.exp2(14.0 - e), (8, T))[None]
        msg[pl.ds(tiles_in * T, PAD), :] = jnp.broadcast_to(e, (PAD, T)).astype(jnp.int32).astype(jnp.int16)

        def one(i, carry):
            a = part[place(row, i), :].reshape(T // 8, 8, T)
            a = jnp.round(a * scale).reshape(T, T)
            msg[rows_of(i * T, T), :] = a.astype(jnp.int32).astype(jnp.int16)
            return carry

        lax.fori_loop(0, tiles_in, one, 0)


    planes = {}

    def plane_start(hop):
        own = panel.at[hop, z, x, y]
        for k, (dy, dx) in enumerate(y_plane):
            planes[hop, -dy % NY, dx] = remote(own, own, in_y(dy, dx))
            planes[hop, -dy % NY, dx].start()

    def plane_wait(hop, dx):
        for d in range(1 - dx, NY):
            slot = panel.at[hop, z, 1 - x if dx else x, rem(y + d, NY)]
            landed(slot, planes[hop, d, dx])

    rings, crossed = {}, {}

    def ring(hop, i, s):
        xx = x if i < 2 else 1 - x
        part_of = pl.ds(2 * (i % 2), 2)
        if s > 1:
            for copy in rings[hop, i, s - 1]:
                copy.wait_recv()
        blocks = [rem(z - (s - 1), NZ), rem(z + (s - 1), NZ)]
        up, down = [panel.at[hop, b, xx, part_of] for b in blocks]
        pairs = [(up, zp), (down, zm)]
        if s == NZ // 2:
            half = panel.at[hop, blocks[0], xx, pl.ds(2 * (i % 2), 1)], panel.at[hop, blocks[1], xx, pl.ds(2 * (i % 2) + 1, 1)]
            pairs = [(half[0], zp), (half[1], zm)]
        rings[hop, i, s] = [remote(block, block, peer) for block, peer in pairs]
        for copy in rings[hop, i, s]:
            copy.start()
        if i == 0 and s > 1:
            cross(hop, s - 1)

    def cross(hop, s):
        part_of = pl.ds(0, 2)
        blocks = [rem(z - s, NZ), rem(z + s, NZ)]
        if s == NZ // 2:
            blocks = blocks[:1]
        crossed[hop, s] = [remote(panel.at[hop, b, x, part_of], panel.at[hop, b, x, part_of], at(z, y, 1 - x)) for b in blocks]
        for copy in crossed[hop, s]:
            copy.start()

    def ring_end(hop, i):
        for copy in rings[hop, i, NZ // 2]:
            copy.wait_recv()
        if i == 0:
            cross(hop, NZ // 2)

    def cross_wait(hop, s):
        blocks = [rem(z - s, NZ), rem(z + s, NZ)]
        for b, copy in zip(blocks, crossed[hop, s]):
            landed(panel.at[hop, b, 1 - x, pl.ds(0, 2)], copy)

    def ring_products(hop, i, s):
        xx = 1 - x if i else x
        groups = [rem(z - s, NZ) * 2 + xx, rem(z + s, NZ) * 2 + xx]
        each(product_forward, hop, groups if 0 < s < NZ // 2 else groups[:1])

    forward = {}

    def pack_tile(msg, a):
        m = jnp.max(jnp.abs(a).reshape(T // 8, 8, T), axis=0)
        e = jnp.ceil(jnp.log2(jnp.maximum(jnp.max(m, axis=0, keepdims=True), 1e-30)))
        msg[pl.ds(T, PAD), :] = jnp.broadcast_to(e, (PAD, T)).astype(jnp.int32).astype(jnp.int16)
        scale = jnp.broadcast_to(jnp.exp2(14.0 - e), (8, T))[None]
        a = jnp.round(a.reshape(T // 8, 8, T) * scale).reshape(T, T)
        msg[pl.ds(0, T), :] = a.astype(jnp.int32).astype(jnp.int16)

    def forward_send(hop):
        targets = ((c_far, (1 - xh) * 2 + 1 - core), (c_xh, (1 - xh) * 2 + core), (c_core, xh * 2 + 1 - core))
        forward[hop] = []
        for k, (peer, q) in enumerate(targets):
            pack_tile(s_cols.at[hop, k], acc[rows_of(q * T, T), :])
            copy = remote(s_cols.at[hop, k], r_cols.at[hop, k], peer)
            copy.start()
            forward[hop].append(copy)

    def forward_end(hop):
        mine = acc[rows_of(c * T, T), :]
        t_col = jnp.transpose(jnp.broadcast_to(t_row, (T, T)))
        for k in (2, 1, 0):
            forward[hop][k].wait_recv()
            msg = r_cols.at[hop, k]
            mine = mine + decode(msg, 0, scale_of(msg, T))
        mine = (1.0 - t_col) * mine + t_col * h[...]
        if hop == 0:
            panel[1, z, x, y] = mine.astype(jnp.bfloat16)
        else:
            prop[...] = mine


    queries = {}

    def query_start(hop):
        queries[hop] = [remote(qcat.at[hop, :, lane], qcat.at[hop, :, lane], peer) for peer in (c_far, c_xh, c_core)]
        for copy in queries[hop]:
            copy.start()

    def query_wait(hop):
        for copy in queries[hop]:
            copy.wait_recv()

    reduces = {}

    def pair(j):
        return 2 * rem(zpair + j, 4)

    def reduce_one(hop, j):
        zz = pair(j)
        each(product_adjoint, hop, [zz * 2 + i for i in range(4)])
        for way, peer in ((0, ym), (1, yp)):
            msg = s_one.at[hop, j, way]
            pack_message(msg, tile_row(2, zz, way), 2)
            copy = remote(msg, r_one.at[hop, j, way], peer)
            copy.start()
            reduces[1, hop, j, way] = copy

    def reduce_two(hop, j):
        zz = pair(j)
        for way, peer, dy in ((0, ym, -1), (1, yp, 1)):
            reduces[1, hop, j, way].wait_recv()
            add_message(r_one.at[hop, j, way], tile_row(dy, zz, way), 2)
            msg = s_two.at[hop, j, way]
            pack_message(msg, tile_row(dy, zz, 0), 4)
            copy = remote(msg, r_two.at[hop, j, way], peer)
            copy.start()
            reduces[2, hop, j, way] = copy

    def reduce_x(hop, j):
        zz = pair(j)
        for way in range(2):
            reduces[2, hop, j, way].wait_recv()
            add_message(r_two.at[hop, j, way], tile_row(0, zz, 0), 4)
        msg = s_x.at[hop, j]
        pack_message(msg, tile_row(0, zz, 1 - x), 2)
        reduces[3, hop, j] = remote(msg, r_x.at[hop, j], at(z, y, 1 - x))
        reduces[3, hop, j].start()

    def own_copy(hop, j, i):
        zz = pair(j) + i
        slot = rem(z - zz, NZ)
        copy = pltpu.make_async_remote_copy(
            src_ref=s_own.at[hop, j, i], dst_ref=r_own.at[hop, slot],
            send_sem=so.at[hop, 2 * j + i], recv_sem=ro.at[hop, slot],
            device_id=at(zz, y, x), device_id_type=MESH,
        )
        return copy, slot

    def reduce_own(hop, j):
        zz = pair(j)
        reduces[3, hop, j].wait_recv()
        add_message(r_x.at[hop, j], tile_row(0, zz, x), 2)
        for i in range(2):
            pack_message(s_own.at[hop, j, i], tile_row(0, zz + i, x), 1)
            copy, slot = own_copy(hop, j, i)
            if j:
                copy.start()
            else:
                pl.when(slot != 0)(copy.start)

    def own_done(hop):
        for j in range(4):
            for i in range(2):
                copy, slot = own_copy(hop, j, i)
                if j:
                    copy.wait_send()
                else:
                    pl.when(slot != 0)(copy.wait_send)

    def adjoint_end(hop):
        row = tile_row(0, z, x)
        for slot in (4, 3, 5, 2, 6, 7, 1):
            pltpu.make_async_remote_copy(
                src_ref=r_own.at[hop, slot], dst_ref=r_own.at[hop, slot], send_sem=so.at[hop, 0],
                recv_sem=ro.at[hop, slot], device_id=yp, device_id_type=MESH,
            ).wait_recv()
            add_message(r_own.at[hop, slot], row, 1)

        d = part[rows_of(row, T), :]
        if hop == 0:
            d_one[...] = d
            qcat[1, :, lane] = (keep_row * d).astype(jnp.bfloat16)
        else:
            grad[...] = jnp.transpose(t_row * jnp.transpose(cot[...]) + t_row * d_one[...] + d)

    pl.semaphore_wait(barrier, len(peers))
    plane_start(0)
    query_start(0)
    load.wait()
    tv[0] = jnp.zeros((T, T), jnp.bfloat16)

    def fill(g, carry):
        for q in range(COLS):
            for i in range(4):
                ad[g, q * T:(q + 1) * T, i * T:(i + 1) * T] = tv[inv[q * 64 + g * 4 + i]]
        return carry

    lax.fori_loop(0, GROUPS, fill, 0)

    p = PARTS
    acc[...] = jnp.zeros_like(acc)

    def ring_begin(hop):
        plane_wait(hop, 0)
        ring(hop, 0, 1)
        ring(hop, 1, 1)
        plane_wait(hop, 1)
        ring(hop, 3, 1)

    ring_begin(0)
    query_wait(0)
    for hop in range(2):
        if hop == 0:
            reduce_one(hop, p[0])
            reduce_one(hop, p[1])
        ring_products(hop, 0, 0)
        ring(hop, 0, 2)
        ring(hop, 1, 2)
        if hop == 0:
            reduce_one(hop, p[2])
            reduce_one(hop, p[3])
        ring(hop, 3, 2)
        reduce_two(hop, p[0])
        reduce_two(hop, p[1])
        ring(hop, 0, 3)
        ring(hop, 1, 3)
        ring_products(hop, 1, 0)
        ring_products(hop, 0, 1)
        ring(hop, 3, 3)
        reduce_two(hop, p[2])
        reduce_x(hop, p[0])
        ring(hop, 0, 4)
        ring(hop, 1, 4)
        reduce_two(hop, p[3])
        cross_wait(hop, 1)
        ring_products(hop, 1, 1)
        ring_products(hop, 0, 2)
        ring(hop, 3, 4)
        reduce_x(hop, p[1])
        reduce_own(hop, p[0])
        cross_wait(hop, 2)
        ring_products(hop, 1, 2)
        ring_products(hop, 0, 3)
        ring_end(hop, 0)
        reduce_x(hop, p[2])
        reduce_own(hop, p[1])
        ring_end(hop, 1)
        cross_wait(hop, 3)
        ring_products(hop, 1, 3)
        ring_products(hop, 0, 4)
        reduce_x(hop, p[3])
        ring_end(hop, 3)
        reduce_own(hop, p[2])
        reduce_own(hop, p[3])
        cross_wait(hop, 4)
        ring_products(hop, 1, 4)
        forward_send(hop)
        adjoint_end(hop)
        if hop == 0:
            query_start(1)
        forward_end(hop)
        if hop == 0:
            plane_start(1)
            acc[...] = jnp.zeros_like(acc)
            ring_begin(1)
            query_wait(1)
            for j in p:
                reduce_one(1, j)

    for copy in sent:
        copy.wait_send()
    for hop in range(2):
        own_done(hop)


def hand_over(a, b, prop, grad):
    prop[...] = a[...]
    grad[...] = b[...]


def shards(h_start, cotangent, node_type, teleport, tile_values, tile_row, tile_col, tile_count):
    spot = jnp.arange(COLS * 64, dtype=jnp.int32)[:, None]
    row, col = spot // 64, spot % 64 // 8 * 8 + spot % 4 * 2 + spot // 4 % 2
    slot = jnp.arange(SLOTS, dtype=jnp.int32)[None, :]
    hit = (tile_row[0] == row) & (tile_col[0] == col) & (slot < tile_count)
    inv = jnp.sum(jnp.where(hit, slot + 1, 0), axis=1)

    vmem = pl.BlockSpec(memory_space=pltpu.VMEM)
    smem = pl.BlockSpec(memory_space=pltpu.SMEM)
    tile = jax.ShapeDtypeStruct((T, T), jnp.float32)
    copies = 160
    raw = pl.pallas_call(
        kernel,
        out_shape=(tile, tile),
        in_specs=[smem, smem, pl.BlockSpec(memory_space=pl.ANY)] + [vmem] * 3,
        out_specs=(vmem, vmem),
        scratch_shapes=[
            pltpu.VMEM((SLOTS + 1, T, T), jnp.bfloat16),
            pltpu.VMEM((GROUPS, 512, 512), jnp.bfloat16),
            pltpu.VMEM((2, NZ, NX, NY, T, T), jnp.bfloat16),
            pltpu.VMEM((64 * T, T), jnp.float32),
            pltpu.VMEM((2, T, COLS * T), jnp.bfloat16),
            pltpu.VMEM((COLS * T, T), jnp.float32),
            pltpu.VMEM((2, 3, T + PAD, T), jnp.int16),
            pltpu.VMEM((2, 3, T + PAD, T), jnp.int16),
            pltpu.VMEM((2, 4, 2, 2 * T + PAD, T), jnp.int16),
            pltpu.VMEM((2, 4, 2, 2 * T + PAD, T), jnp.int16),
            pltpu.VMEM((2, 4, 2, 4 * T + PAD, T), jnp.int16),
            pltpu.VMEM((2, 4, 2, 4 * T + PAD, T), jnp.int16),
            pltpu.VMEM((2, 4, 2 * T + PAD, T), jnp.int16),
            pltpu.VMEM((2, 4, 2 * T + PAD, T), jnp.int16),
            pltpu.VMEM((2, 4, 2, T + PAD, T), jnp.int16),
            pltpu.VMEM((2, NZ, T + PAD, T), jnp.int16),
            pltpu.VMEM((T, T), jnp.float32),
            pltpu.SemaphoreType.DMA,
            pltpu.SemaphoreType.DMA((copies,)),
            pltpu.SemaphoreType.DMA((copies,)),
            pltpu.SemaphoreType.DMA((2, NZ)),
            pltpu.SemaphoreType.DMA((2, NZ)),
        ],
        compiler_params=pltpu.CompilerParams(
            collective_id=0, has_side_effects=True, vmem_limit_bytes=56 << 20
        ),
    )(inv, teleport, tile_values[0, 0], h_start, cotangent, node_type[None, :])
    return pl.pallas_call(
        hand_over,
        out_shape=(tile, tile),
        in_specs=[vmem, vmem],
        out_specs=(vmem, vmem),
    )(*raw)


def solution(mesh):
    placed = (
        P(("rows", "cols"), None),
        P(("rows", "cols"), None),
        P(("rows", "cols")),
        P(),
        P("rows", "cols", None, None, None),
        P("rows", "cols", None),
        P("rows", "cols", None),
        P("rows", "cols"),
    )
    return jax.shard_map(
        shards,
        mesh=mesh,
        in_specs=placed,
        out_specs=(P(("rows", "cols"), None), P(("rows", "cols"), None)),
        check_vma=False,
    )
```
